128 devices in a mesh: row: 8 (over x_lo, z), col: 16 (over x_hi, y, core).
Axes of the slice: x: 4 (x_hi: 2, x_lo: 2; x = x_hi * 2 + x_lo), y: 4, z: 4, core: 2. Of those that a mesh axis runs over, the one named last changes fastest.
Arguments:
- inputs: bfloat16 [512, 8192], P(None, 'row'), may hold values from -6 to 6
- up_weight: bfloat16 [8192, 28672], P('row', 'col'), may hold values from -0.109375 to 0.109375
- down_weight: bfloat16 [28672, 8192], P('col', 'row'), may hold values from -0.0546875 to 0.0546875
- up_mask: int32 [64, 224], P('row', 'col'), may hold values 0 or 1
- down_mask: int32 [224, 64], P('col', 'row'), may hold values 0 or 1
- cotangent: bfloat16 [512, 8192], P(None, 'row'), may hold values from -6 to 6
Outputs:
- output: bfloat16 [512, 8192], P(None, 'row')
- input_grad: bfloat16 [512, 8192], P(None, 'row')
- up_grad: bfloat16 [8192, 28672], P('row', 'col')
- down_grad: bfloat16 [28672, 8192], P('col', 'row')
The draws below stay inside these ranges and needn't reach their ends.
All inputs are finite; a program needn't handle non-finite values. No bound on the sum of `up_mask` or of `down_mask` on one device may be relied on, other than what follows from the above.
Results may differ from the reference program's by a relative error of at most 0.0051.
Values may be sent and summed in bfloat16 or wider, within the bound.
No kernel may reach another device: no remote copies, remote signals or barrier semaphores. Data moves between devices by JAX's collectives and lax.ppermute only.
A program may use at most 128 MiB of HBM per device.

```python
import jax
import jax.numpy as jnp

D = 8192
FF = 28672
BLK = 128
TOKENS = 512


def touch_ends(drawn, rng, smallest, top_value):
    shape = drawn.shape
    spot = [jax.random.randint(jax.random.fold_in(rng, axis), (), 0, shape[axis]) for axis in range(len(shape))]
    drawn = drawn.at[tuple(spot)].set(smallest)
    longest = shape.index(max(shape))
    spot[longest] = (spot[longest] + 1) % shape[longest]
    return drawn.at[tuple(spot)].set(top_value)


def shard_levels(key, dims, shards, smallest, top_value):
    factor_of, own = 1.0, jax.random.fold_in(key, 6)
    for dim, blocks in shards:
        heights = jnp.exp(jax.random.uniform(jax.random.fold_in(own, dim), (blocks,), jnp.float32, smallest / len(shards), top_value / len(shards)))
        factor_of = factor_of * jnp.repeat(heights, dims[dim] // blocks).reshape([-1 if axis == dim else 1 for axis in range(len(dims))])
    return factor_of


def centred(key, shape, spread, most, shards=(), dtype=jnp.bfloat16):
    values = jax.random.normal(key, shape, jnp.float32) * spread
    if len(shards) > 0:
        values = shard_levels(key, shape, shards, -0.22, 0.18) * values
    return jnp.clip(values, min=-most, max=most).astype(dtype)


def setup_inputs(seed: int = 0) -> dict:
    arg_keys = jax.random.split(jax.random.key(seed), 7)
    return {
        "inputs": centred(arg_keys[0], (TOKENS, D), 1.0, 6.0, ((1, 8),)),
        "up_weight": centred(arg_keys[1], (D, FF), (D * 2 // 5) ** -0.5, 0.109375, ((0, 8), (1, 16))),
        "down_weight": centred(arg_keys[2], (FF, D), (FF * 2 // 5) ** -0.5, 0.0546875, ((0, 16), (1, 8))),
        "up_mask": touch_ends((jax.random.randint(arg_keys[3], (D // BLK, FF // BLK), 0, 5) < 2).astype(jnp.int32), jax.random.fold_in(arg_keys[3], 1), 0, 1),
        "down_mask": touch_ends((jax.random.randint(arg_keys[4], (FF // BLK, D // BLK), 0, 5) < 2).astype(jnp.int32), jax.random.fold_in(arg_keys[4], 1), 0, 1),
        "cotangent": centred(arg_keys[5], (TOKENS, D), 1.0, 6.0, ((1, 8),)),
    }


def expand(mask, block):
    kept = mask > 0
    return jnp.repeat(jnp.repeat(kept, block, axis=0), block, axis=1)

def activate(value):
    return jax.nn.gelu(value, approximate=True)

def reference(inputs, up_weight, down_weight, up_mask, down_mask, cotangent):
    block = up_weight.shape[0] // up_mask.shape[0]
    keep_up = expand(up_mask, block)
    keep_down = expand(down_mask, block)
    masked_up = jnp.where(keep_up, up_weight, jnp.zeros_like(up_weight))
    masked_down = jnp.where(keep_down, down_weight, jnp.zeros_like(down_weight))
    hidden = jnp.dot(inputs, masked_up, preferred_element_type=jnp.float32)
    active_full, pull_back = jax.vjp(activate, hidden)
    active = active_full.astype(jnp.bfloat16)
    output = jnp.dot(active, masked_down, preferred_element_type=jnp.float32).astype(jnp.bfloat16)
    active_grad = jnp.dot(cotangent, masked_down.T, preferred_element_type=jnp.float32)
    hidden_grad = pull_back(active_grad)[0].astype(jnp.bfloat16)
    input_grad = jnp.dot(hidden_grad, masked_up.T, preferred_element_type=jnp.float32).astype(jnp.bfloat16)
    up_full = jnp.dot(inputs.T, hidden_grad, preferred_element_type=jnp.float32)
    up_grad = jnp.where(keep_up, up_full, jnp.zeros_like(up_full)).astype(jnp.bfloat16)
    down_full = jnp.dot(active.T, cotangent, preferred_element_type=jnp.float32)
    down_grad = jnp.where(keep_down, down_full, jnp.zeros_like(down_full)).astype(jnp.bfloat16)
    return (output, input_grad, up_grad, down_grad)
```

```python
import jax
import jax.numpy as jnp
from jax import lax
from jax.sharding import PartitionSpec as P

F32 = jnp.float32
BF16 = jnp.bfloat16


def z_step(d):
    return [(x * 4 + z, x * 4 + (z + d) % 4) for x in range(2) for z in range(4)]


def y_step(d):
    return [(h * 8 + y * 2 + c, h * 8 + (y + d) % 4 * 2 + c) for h in range(2) for y in range(4) for c in range(2)]


X_SWAP = [(i, i ^ 4) for i in range(8)]
CORE_SWAP = [(i, i ^ 1) for i in range(16)]
H_SWAP = [(i, i ^ 8) for i in range(16)]


def row_send(v, perm):
    return lax.ppermute(v, "row", perm)


def col_send(v, perm):
    return lax.ppermute(v, "col", perm)


def rolled(array, start, count):
    size = array.shape[0] // count
    twice = jnp.concatenate([array, array], axis=0)
    return lax.dynamic_slice_in_dim(twice, start * size, array.shape[0], 0)


def expand(mask, block):
    kept = mask > 0
    return jnp.repeat(jnp.repeat(kept, block, axis=0), block, axis=1)


def activate(value):
    return jax.nn.gelu(value, approximate=True)


def z_reduce(part):
    own, nxt, far, prv = jnp.split(part, 4, axis=0)
    half = own.shape[0] // 2
    from_prv = row_send(far[:half].astype(BF16), z_step(1))
    from_nxt = row_send(far[half:].astype(BF16), z_step(-1))
    up = jnp.concatenate([nxt[:half] + from_prv.astype(F32), nxt[half:]], axis=0).astype(BF16)
    down = jnp.concatenate([prv[:half], prv[half:] + from_nxt.astype(F32)], axis=0).astype(BF16)
    a = row_send(up, z_step(1))
    b = row_send(down, z_step(-1))
    return own + a.astype(F32) + b.astype(F32)


def x_reduce(part):
    return part + row_send(part.astype(BF16), X_SWAP).astype(F32)


def z_collect(own):
    half = own.shape[0] // 2
    prv = row_send(own, z_step(1))
    nxt = row_send(own, z_step(-1))
    far_a = row_send(nxt[:half], z_step(-1))
    far_b = row_send(prv[half:], z_step(1))
    return jnp.concatenate([own, nxt, far_a, far_b, prv], axis=0)


def col_reduce(part, z):
    col = lax.axis_index("col")
    core, y = col % 2, col // 2 % 4
    rows = part.shape[0]
    kept = lax.dynamic_slice_in_dim(part, core * (rows // 2), rows // 2, 0)
    sent = lax.dynamic_slice_in_dim(part, (1 - core) * (rows // 2), rows // 2, 0).astype(BF16)
    mine = kept + col_send(sent, CORE_SWAP).astype(F32)
    own, nxt, far, prv = jnp.split(rolled(mine, y, 4), 4, axis=0)
    own = own + col_send(nxt.astype(BF16), y_step(1)).astype(F32)
    own = own + col_send(prv.astype(BF16), y_step(-1)).astype(F32)
    own = own + col_send(far.astype(BF16), y_step(2)).astype(F32)
    own = own.astype(BF16)
    own = (own.astype(F32) + col_send(own, H_SWAP).astype(F32)).astype(BF16)
    prv = col_send(own, y_step(1))
    nxt = col_send(own, y_step(-1))
    far = col_send(own, y_step(2))
    mine = rolled(jnp.concatenate([own, nxt, far, prv], axis=0), (4 - y) % 4, 4)
    other = col_send(mine, CORE_SWAP)
    both = rolled(jnp.concatenate([mine, other], axis=0), core, 2)
    return rolled(both, (4 - z) % 4, 4)


def body(inputs, up_weight, down_weight, up_mask, down_mask, cotangent):
    block = up_weight.shape[0] // up_mask.shape[0]
    z = lax.axis_index("row") % 4
    inputs = rolled(inputs, z, 4)
    cotangent = rolled(cotangent, z, 4)
    keep_up = expand(up_mask, block)
    keep_down = expand(down_mask, block)
    masked_up = jnp.where(keep_up, up_weight, jnp.zeros_like(up_weight))
    masked_down = jnp.where(keep_down, down_weight, jnp.zeros_like(down_weight))
    hidden_part = jnp.dot(inputs, masked_up, preferred_element_type=F32)
    hidden = x_reduce(z_reduce(hidden_part))
    active_own, pull_back = jax.vjp(activate, hidden)
    active = z_collect(active_own.astype(BF16))
    grad_part = jnp.dot(cotangent, masked_down.T, preferred_element_type=F32)
    grad = x_reduce(z_reduce(grad_part))
    hidden_grad = z_collect(pull_back(grad)[0].astype(BF16))
    output_part = jnp.dot(active, masked_down, preferred_element_type=F32)
    output = col_reduce(output_part, z)
    input_part = jnp.dot(hidden_grad, masked_up.T, preferred_element_type=F32)
    input_grad = col_reduce(input_part, z)
    up_full = jnp.dot(inputs.T, hidden_grad, preferred_element_type=F32)
    up_grad = jnp.where(keep_up, up_full, jnp.zeros_like(up_full)).astype(BF16)
    down_full = jnp.dot(active.T, cotangent, preferred_element_type=F32)
    down_grad = jnp.where(keep_down, down_full, jnp.zeros_like(down_full)).astype(BF16)
    return (output, input_grad, up_grad, down_grad)


def solution(mesh):
    in_specs = (
        P(None, "row"),
        P("row", "col"),
        P("col", "row"),
        P("row", "col"),
        P("col", "row"),
        P(None, "row"),
    )
    out_specs = (P(None, "row"), P(None, "row"), P("row", "col"), P("col", "row"))
    return jax.shard_map(body, mesh=mesh, in_specs=in_specs, out_specs=out_specs, check_vma=False)
```

```python
import functools

import jax
import jax.numpy as jnp
from jax import lax
from jax.experimental import pallas as pl
from jax.experimental.pallas import tpu as pltpu
from jax.sharding import PartitionSpec as P

F32 = jnp.float32
BF16 = jnp.bfloat16
BLOCK = 128
TILE = 256


def z_step(d):
    return [(x * 4 + z, x * 4 + (z + d) % 4) for x in range(2) for z in range(4)]


def y_step(d):
    return [(h * 8 + y * 2 + c, h * 8 + (y + d) % 4 * 2 + c) for h in range(2) for y in range(4) for c in range(2)]


X_SWAP = [(i, i ^ 4) for i in range(8)]
CORE_SWAP = [(i, i ^ 1) for i in range(16)]
H_SWAP = [(i, i ^ 8) for i in range(16)]


def row_send(v, perm):
    return lax.ppermute(v, "row", perm)


def col_send(v, perm):
    return lax.ppermute(v, "col", perm)


def whole(shape):
    return pl.BlockSpec(shape, lambda *_: (0,) * len(shape))


def masked(w, mask_ref, row0, col0):
    rows = []
    for r in range(w.shape[0] // BLOCK):
        row = w[r * BLOCK : (r + 1) * BLOCK]
        cols = []
        for c in range(w.shape[1] // BLOCK):
            piece = row[:, c * BLOCK : (c + 1) * BLOCK]
            cols.append(jnp.where(mask_ref[row0 + r, col0 + c] > 0, piece, jnp.zeros_like(piece)))
        rows.append(jnp.concatenate(cols, axis=1))
    return jnp.concatenate(rows, axis=0)


def dims(lhs, rhs):
    return (((lhs,), (rhs,)), ((), ()))


def call(body, name, grid, in_specs, out_specs, out_shape, scratch=(), prefetch=2):
    return pl.pallas_call(
        body,
        name=name,
        grid_spec=pltpu.PrefetchScalarGridSpec(
            num_scalar_prefetch=prefetch, grid=grid, in_specs=in_specs, out_specs=out_specs, scratch_shapes=scratch
        ),
        out_shape=out_shape,
        compiler_params=pltpu.CompilerParams(vmem_limit_bytes=50 * 1024 * 1024),
    )


def split_part(pos, mask, x, w, transposed):
    units = w.shape[0] if transposed else w.shape[1]
    tokens = x.shape[0] // 4
    half = tokens // 2

    def kernel(pos_ref, mask_ref, x_ref, w_ref, far_a, far_b, own, nxt, prv, acc):
        j = pl.program_id(0) * (TILE // BLOCK)
        z = pos_ref[0]
        if transposed:
            tile = masked(w_ref[...], mask_ref, j, 0)
            acc[...] = lax.dot_general(x_ref[...], tile, dims(1, 1), preferred_element_type=F32)
        else:
            tile = masked(w_ref[...], mask_ref, 0, j)
            acc[...] = lax.dot_general(x_ref[...], tile, dims(1, 0), preferred_element_type=F32)

        def rows(k):
            return acc[pl.ds(pl.multiple_of((z + k) % 4 * tokens, tokens), tokens), :]

        own[...] = rows(0)
        nxt[...] = rows(1)
        far = rows(2).astype(BF16)
        far_a[...] = far[:half]
        far_b[...] = far[half:]
        prv[...] = rows(3)

    def out(rows):
        return pl.BlockSpec((rows, TILE), lambda j, *_: (0, j))

    w_spec = (
        pl.BlockSpec((TILE, w.shape[1]), lambda j, *_: (j, 0))
        if transposed
        else pl.BlockSpec((w.shape[0], TILE), lambda j, *_: (0, j))
    )
    shapes = [jax.ShapeDtypeStruct((half, units), BF16)] * 2 + [jax.ShapeDtypeStruct((tokens, units), F32)] * 3
    return call(
        kernel, "grad_part" if transposed else "hidden_part", (units // TILE,), [whole(x.shape), w_spec],
        [out(half)] * 2 + [out(tokens)] * 3, shapes, [pltpu.VMEM((x.shape[0], TILE), F32)],
    )(pos, mask, x, w)


def joined(nxt, prv, from_prv, from_nxt):
    tokens, units = nxt.shape
    half = tokens // 2

    def kernel(nxt_ref, prv_ref, a_ref, b_ref, up, down):
        up[:half] = (nxt_ref[:half] + a_ref[...].astype(F32)).astype(BF16)
        up[half:] = nxt_ref[half:].astype(BF16)
        down[:half] = prv_ref[:half].astype(BF16)
        down[half:] = (prv_ref[half:] + b_ref[...].astype(F32)).astype(BF16)

    wide = units // 2
    full = pl.BlockSpec((tokens, wide), lambda j: (0, j))
    part = pl.BlockSpec((half, wide), lambda j: (0, j))
    return call(
        kernel, "joined", (2,), [full, full, part, part], [full, full],
        [jax.ShapeDtypeStruct((tokens, units), BF16)] * 2, prefetch=0,
    )(nxt, prv, from_prv, from_nxt)


def z_reduce(pieces):
    far_a, far_b, own, nxt, prv = pieces
    from_prv = row_send(far_a, z_step(1))
    from_nxt = row_send(far_b, z_step(-1))
    up, down = joined(nxt, prv, from_prv, from_nxt)
    a = row_send(up, z_step(1))
    b = row_send(down, z_step(-1))
    return own + a.astype(F32) + b.astype(F32)


def x_reduce(part):
    return part + row_send(part.astype(BF16), X_SWAP).astype(F32)


def z_collect(own):
    half = own.shape[0] // 2
    prv = row_send(own, z_step(1))
    nxt = row_send(own, z_step(-1))
    far_a = row_send(nxt[:half], z_step(-1))
    far_b = row_send(prv[half:], z_step(1))
    return own, nxt, far_a, far_b, prv


def gather_rows(refs, scratch):
    at = 0
    for ref in refs:
        scratch[at : at + ref.shape[0]] = ref[...]
        at += ref.shape[0]


def down_part(pos, mask, pieces, w, transposed):
    width = w.shape[0] if transposed else w.shape[1]
    units = w.shape[1] if transposed else w.shape[0]
    tokens = sum(p.shape[0] for p in pieces)
    half, quarter = tokens // 2, tokens // 8

    def kernel(pos_ref, mask_ref, *refs):
        parts, (w_ref, kept, sent, lhs, acc) = refs[: len(pieces)], refs[len(pieces) :]
        j = pl.program_id(0)

        @pl.when(j == 0)
        def _():
            gather_rows(parts, lhs)

        j = j * (TILE // BLOCK)
        y, core = pos_ref[1], pos_ref[2]
        if transposed:
            tile = masked(w_ref[...], mask_ref, j, 0)
            acc[...] = lax.dot_general(lhs[...], tile, dims(1, 1), preferred_element_type=F32)
        else:
            tile = masked(w_ref[...], mask_ref, 0, j)
            acc[...] = lax.dot_general(lhs[...], tile, dims(1, 0), preferred_element_type=F32)
        for k in range(4):
            at = (y + k) % 4 * quarter
            here = pl.multiple_of(core * half + at, quarter)
            there = pl.multiple_of((1 - core) * half + at, quarter)
            kept[k * quarter : (k + 1) * quarter] = acc[pl.ds(here, quarter), :]
            sent[k * quarter : (k + 1) * quarter] = acc[pl.ds(there, quarter), :].astype(BF16)

    w_spec = (
        pl.BlockSpec((TILE, units), lambda j, *_: (j, 0))
        if transposed
        else pl.BlockSpec((units, TILE), lambda j, *_: (0, j))
    )
    out = pl.BlockSpec((half, TILE), lambda j, *_: (0, j))
    return call(
        kernel, "input_part" if transposed else "output_part", (width // TILE,),
        [whole(p.shape) for p in pieces] + [w_spec], [out, out],
        [jax.ShapeDtypeStruct((half, width), F32), jax.ShapeDtypeStruct((half, width), BF16)],
        [pltpu.VMEM((tokens, units), BF16), pltpu.VMEM((tokens, TILE), F32)],
    )(pos, mask, *pieces, w)


def up_gradient(pos, mask, x, pieces):
    tokens, width = x.shape
    units = pieces[0].shape[1]
    size = tokens // 4

    def kernel(pos_ref, mask_ref, x_ref, *refs):
        parts, (out, lhs, rhs) = refs[: len(pieces)], refs[len(pieces) :]
        j = pl.program_id(0)

        @pl.when(j == 0)
        def _():
            for k in range(4):
                at = pl.multiple_of((pos_ref[0] + k) % 4 * size, size)
                lhs[:, k * size : (k + 1) * size] = x_ref[pl.ds(at, size), :].T

        gather_rows(parts, rhs)
        full = lax.dot_general(lhs[...], rhs[...], dims(1, 0), preferred_element_type=F32)
        out[...] = masked(full, mask_ref, 0, j * (TILE // BLOCK)).astype(BF16)

    return call(
        kernel, "up_grad", (units // TILE,),
        [whole(x.shape)] + [pl.BlockSpec((p.shape[0], TILE), lambda j, *_: (0, j)) for p in pieces],
        pl.BlockSpec((width, TILE), lambda j, *_: (0, j)), jax.ShapeDtypeStruct((width, units), BF16),
        [pltpu.VMEM((width, tokens), BF16), pltpu.VMEM((tokens, TILE), BF16)],
    )(pos, mask, x, *pieces)


def down_gradient(pos, mask, pieces, x):
    tokens, width = x.shape
    units = pieces[0].shape[1]
    size = tokens // 4

    def kernel(pos_ref, mask_ref, *refs):
        parts, (x_ref, out, lhs, rhs) = refs[: len(pieces)], refs[len(pieces) :]
        j = pl.program_id(0)

        @pl.when(j == 0)
        def _():
            for k in range(4):
                at = pl.multiple_of((pos_ref[0] + k) % 4 * size, size)
                rhs[k * size : (k + 1) * size] = x_ref[pl.ds(at, size), :]

        gather_rows(parts, lhs)
        full = lax.dot_general(lhs[...], rhs[...], dims(0, 0), preferred_element_type=F32)
        out[...] = masked(full, mask_ref, j * (TILE // BLOCK), 0).astype(BF16)

    return call(
        kernel, "down_grad", (units // TILE,),
        [pl.BlockSpec((p.shape[0], TILE), lambda j, *_: (0, j)) for p in pieces] + [whole(x.shape)],
        pl.BlockSpec((TILE, width), lambda j, *_: (j, 0)), jax.ShapeDtypeStruct((units, width), BF16),
        [pltpu.VMEM((tokens, TILE), BF16), pltpu.VMEM((tokens, width), BF16)],
    )(pos, mask, *pieces, x)


def y_joined(pos, pieces):
    size, width = pieces[0].shape

    def kernel(pos_ref, *refs):
        for k in range(4):
            at = pl.multiple_of((pos_ref[1] + k) % 4 * size, size)
            refs[4][pl.ds(at, size), :] = refs[k][...]

    spec = whole((size, width))
    return call(
        kernel, "y_joined", (1,), [spec] * 4, whole((4 * size, width)),
        jax.ShapeDtypeStruct((4 * size, width), BF16), prefetch=1,
    )(pos, *pieces)


def all_rows(pos, mine, other):
    half, width = mine.shape
    size = half // 2

    def kernel(pos_ref, mine_ref, other_ref, out):
        z, core = pos_ref[0], pos_ref[2]
        for k in range(2):
            here = pl.multiple_of((z + 2 * core + k) % 4 * size, size)
            there = pl.multiple_of((z + 2 * (1 - core) + k) % 4 * size, size)
            out[pl.ds(here, size), :] = mine_ref[k * size : (k + 1) * size]
            out[pl.ds(there, size), :] = other_ref[k * size : (k + 1) * size]

    return call(
        kernel, "all_rows", (1,), [whole(mine.shape)] * 2, whole((2 * half, width)),
        jax.ShapeDtypeStruct((2 * half, width), BF16), prefetch=1,
    )(pos, mine, other)


def col_reduce(pos, kept, sent):
    mine = kept + col_send(sent, CORE_SWAP).astype(F32)
    own, nxt, far, prv = jnp.split(mine, 4, axis=0)
    a = col_send(far.astype(BF16), y_step(2))
    b = col_send(nxt.astype(BF16), y_step(1))
    c = col_send(prv.astype(BF16), y_step(-1))
    own = (own + a.astype(F32) + b.astype(F32) + c.astype(F32)).astype(BF16)
    own = (own.astype(F32) + col_send(own, H_SWAP).astype(F32)).astype(BF16)
    far = col_send(own, y_step(2))
    prv = col_send(own, y_step(1))
    nxt = col_send(own, y_step(-1))
    mine = y_joined(pos, (own, nxt, far, prv))
    return all_rows(pos, mine, col_send(mine, CORE_SWAP))


def activate(value):
    return jax.nn.gelu(value, approximate=True)


def body(inputs, up_weight, down_weight, up_mask, down_mask, cotangent):
    col = lax.axis_index("col")
    pos = jnp.stack([lax.axis_index("row") % 4, col // 2 % 4, col % 2]).astype(jnp.int32)
    hidden = x_reduce(z_reduce(split_part(pos, up_mask, inputs, up_weight, False)))
    active_own, pull_back = jax.vjp(activate, hidden)
    active = z_collect(active_own.astype(BF16))
    grad = x_reduce(z_reduce(split_part(pos, down_mask, cotangent, down_weight, True)))
    hidden_grad = z_collect(pull_back(grad)[0].astype(BF16))
    output = col_reduce(pos, *down_part(pos, down_mask, active, down_weight, False))
    input_grad = col_reduce(pos, *down_part(pos, up_mask, hidden_grad, up_weight, True))
    down_grad = down_gradient(pos, down_mask, active, cotangent)
    up_grad = up_gradient(pos, up_mask, inputs, hidden_grad)
    return (output, input_grad, up_grad, down_grad)


def solution(mesh):
    in_specs = (
        P(None, "row"),
        P("row", "col"),
        P("col", "row"),
        P("row", "col"),
        P("col", "row"),
        P(None, "row"),
    )
    out_specs = (P(None, "row"), P(None, "row"), P("row", "col"), P("col", "row"))
    return jax.shard_map(body, mesh=mesh, in_specs=in_specs, out_specs=out_specs, check_vma=False)
```

```python
import jax
import jax.numpy as jnp
from jax import lax
from jax.experimental import pallas as pl
from jax.experimental.pallas import tpu as pltpu
from jax.sharding import PartitionSpec as P


F32 = jnp.float32
BF16 = jnp.bfloat16
BLOCK = 128


def z_step(d):
    return [(x * 4 + z, x * 4 + (z + d) % 4) for x in range(2) for z in range(4)]


def y_step(d):
    return [(h * 8 + y * 2 + c, h * 8 + (y + d) % 4 * 2 + c) for h in range(2) for y in range(4) for c in range(2)]


X_SWAP = [(i, i ^ 4) for i in range(8)]
CORE_SWAP = [(i, i ^ 1) for i in range(16)]
H_SWAP = [(i, i ^ 8) for i in range(16)]


def row_send(v, perm):
    return lax.ppermute(v, "row", perm)


def col_send(v, perm):
    return lax.ppermute(v, "col", perm)


def masked(w, mask_ref, row0, col0):
    rows = []
    for r in range(w.shape[0] // BLOCK):
        row = w[r * BLOCK : (r + 1) * BLOCK]
        cols = []
        for c in range(w.shape[1] // BLOCK):
            piece = row[:, c * BLOCK : (c + 1) * BLOCK]
            cols.append(jnp.where(mask_ref[row0 + r, col0 + c] > 0, piece, jnp.zeros_like(piece)))
        rows.append(jnp.concatenate(cols, axis=1))
    return jnp.concatenate(rows, axis=0)


def dims(lhs, rhs):
    return (((lhs,), (rhs,)), ((), ()))


VMEM = pl.BlockSpec(memory_space=pltpu.VMEM)
SMEM = pl.BlockSpec(memory_space=pltpu.SMEM)
HBM = pl.BlockSpec(memory_space=pl.ANY)
CHUNK = 256


def call(body, in_specs, out_specs, out_shape, scratch=()):
    return pl.pallas_call(
        body,
        in_specs=in_specs,
        out_specs=out_specs,
        out_shape=out_shape,
        scratch_shapes=scratch,
        compiler_params=pltpu.CompilerParams(vmem_limit_bytes=50 * 1024 * 1024),
    )


def chunk_of(ref, i, rows):
    at = pl.ds(i * CHUNK, CHUNK)
    return ref.at[at, :] if rows else ref.at[:, at]


def fetches(src, dst, sems, rows):
    count = src.shape[0 if rows else 1] // CHUNK
    return [pltpu.make_async_copy(chunk_of(src, i, rows), chunk_of(dst, i, rows), sems.at[i]) for i in range(count)]


def times_chunk(lhs, w, mask_ref, i, rows):
    first = i * (CHUNK // BLOCK)
    tile = masked(chunk_of(w, i, rows)[...], mask_ref, *((first, 0) if rows else (0, first)))
    return lax.dot_general(lhs, tile, dims(1, 1 if rows else 0), preferred_element_type=F32)


def split_part(pos, mask, x, w, transposed):
    units = w.shape[0] if transposed else w.shape[1]
    tokens = x.shape[0] // 4
    half = tokens // 2
    count = units // CHUNK

    def kernel(pos_ref, mask_ref, x_hbm, w_hbm, far_a, far_b, own, nxt, prv, x_ref, w_ref, acc, sems):
        x_copy = pltpu.make_async_copy(x_hbm, x_ref, sems.at[count])
        x_copy.start()
        copies = fetches(w_hbm, w_ref, sems, transposed)
        for copy in copies:
            copy.start()
        x_copy.wait()
        z = pos_ref[0]

        def rows(i, k):
            return acc[i % 2, pl.ds(pl.multiple_of((z + k) % 4 * tokens, tokens), tokens), :]

        for i, copy in enumerate(copies):
            copy.wait()
            acc[i % 2] = times_chunk(x_ref[...], w_ref, mask_ref, i, transposed)
            at = pl.ds(i * CHUNK, CHUNK)
            own[:, at] = rows(i, 0)
            nxt[:, at] = rows(i, 1)
            far = rows(i, 2).astype(BF16)
            far_a[:, at] = far[:half]
            far_b[:, at] = far[half:]
            prv[:, at] = rows(i, 3)

    shapes = [jax.ShapeDtypeStruct((half, units), BF16)] * 2 + [jax.ShapeDtypeStruct((tokens, units), F32)] * 3
    return call(
        kernel, [SMEM, SMEM, HBM, HBM], [VMEM] * 5, shapes,
        [pltpu.VMEM(x.shape, BF16), pltpu.VMEM(w.shape, BF16), pltpu.VMEM((2, x.shape[0], CHUNK), F32),
         pltpu.SemaphoreType.DMA((count + 1,))],
    )(pos, mask, x, w)


def joined(nxt, prv, from_prv, from_nxt):
    tokens, units = nxt.shape
    half = tokens // 2

    def kernel(nxt_ref, prv_ref, a_ref, b_ref, up, down):
        up[:half] = (nxt_ref[:half] + a_ref[...].astype(F32)).astype(BF16)
        up[half:] = nxt_ref[half:].astype(BF16)
        down[:half] = prv_ref[:half].astype(BF16)
        down[half:] = (prv_ref[half:] + b_ref[...].astype(F32)).astype(BF16)

    return call(
        kernel, [VMEM] * 4, [VMEM] * 2, [jax.ShapeDtypeStruct((tokens, units), BF16)] * 2
    )(nxt, prv, from_prv, from_nxt)


def z_reduce(pieces):
    far_a, far_b, own, nxt, prv = pieces
    from_prv = row_send(far_a, z_step(1))
    from_nxt = row_send(far_b, z_step(-1))
    up, down = joined(nxt, prv, from_prv, from_nxt)
    a = row_send(up, z_step(1))
    b = row_send(down, z_step(-1))
    return own + a.astype(F32) + b.astype(F32)


def x_swap(part):
    return row_send(part.astype(BF16), X_SWAP)


def z_collect(own):
    half = own.shape[0] // 2
    prv = row_send(own, z_step(1))
    nxt = row_send(own, z_step(-1))
    far_a = row_send(nxt[:half], z_step(-1))
    far_b = row_send(prv[half:], z_step(1))
    return own, nxt, far_a, far_b, prv


def gather_rows(refs, scratch):
    at = 0
    for ref in refs:
        scratch[at : at + ref.shape[0]] = ref[...]
        at += ref.shape[0]


def down_part(pos, mask, pieces, w, transposed):
    width = w.shape[0] if transposed else w.shape[1]
    units = w.shape[1] if transposed else w.shape[0]
    tokens = sum(p.shape[0] for p in pieces)
    half, quarter = tokens // 2, tokens // 8
    count = width // CHUNK

    def kernel(pos_ref, mask_ref, *refs):
        parts, (w_hbm, kept, sent, w_ref, lhs, acc, sems) = refs[: len(pieces)], refs[len(pieces) :]
        copies = fetches(w_hbm, w_ref, sems, transposed)
        for copy in copies:
            copy.start()
        gather_rows(parts, lhs)
        y, core = pos_ref[1], pos_ref[2]
        for i, copy in enumerate(copies):
            copy.wait()
            acc[i % 2] = times_chunk(lhs[...], w_ref, mask_ref, i, transposed)
            cols = pl.ds(i * CHUNK, CHUNK)
            for k in range(4):
                at = (y + k) % 4 * quarter
                here = pl.multiple_of(core * half + at, quarter)
                there = pl.multiple_of((1 - core) * half + at, quarter)
                to = pl.ds(k * quarter, quarter)
                kept[to, cols] = acc[i % 2, pl.ds(here, quarter), :]
                sent[to, cols] = acc[i % 2, pl.ds(there, quarter), :].astype(BF16)

    return call(
        kernel, [SMEM, SMEM] + [VMEM] * len(pieces) + [HBM], [VMEM] * 2,
        [jax.ShapeDtypeStruct((half, width), F32), jax.ShapeDtypeStruct((half, width), BF16)],
        [pltpu.VMEM(w.shape, BF16), pltpu.VMEM((tokens, units), BF16), pltpu.VMEM((2, tokens, CHUNK), F32),
         pltpu.SemaphoreType.DMA((count,))],
    )(pos, mask, *pieces, w)


def token_rows(pos_ref, x_ref, k):
    size = x_ref.shape[0] // 4
    return x_ref[pl.ds(pl.multiple_of((pos_ref[0] + k) % 4 * size, size), size), :]


def up_gradient(pos, mask, x, pieces):
    tokens, width = x.shape
    units = pieces[0].shape[1]
    size = tokens // 4
    count = units // CHUNK

    def kernel(pos_ref, mask_ref, x_ref, *refs):
        parts, (out, lhs, rhs, result, sems) = refs[: len(pieces)], refs[len(pieces) :]
        for k in range(4):
            lhs[:, k * size : (k + 1) * size] = token_rows(pos_ref, x_ref, k).T
        gather_rows(parts, rhs)
        copies = []
        for i in range(count):
            full = lax.dot_general(
                lhs[...], rhs[:, i * CHUNK : (i + 1) * CHUNK], dims(1, 0), preferred_element_type=F32
            )
            chunk_of(result, i, False)[...] = masked(full, mask_ref, 0, i * (CHUNK // BLOCK)).astype(BF16)
            copies.append(pltpu.make_async_copy(chunk_of(result, i, False), chunk_of(out, i, False), sems.at[i]))
            copies[-1].start()
        for copy in copies:
            copy.wait()

    return call(
        kernel, [SMEM, SMEM, VMEM] + [VMEM] * len(pieces), HBM, jax.ShapeDtypeStruct((width, units), BF16),
        [pltpu.VMEM((width, tokens), BF16), pltpu.VMEM((tokens, units), BF16), pltpu.VMEM((width, units), BF16),
         pltpu.SemaphoreType.DMA((count,))],
    )(pos, mask, x, *pieces)


def down_gradient(pos, mask, pieces, x):
    tokens, width = x.shape
    units = pieces[0].shape[1]
    size = tokens // 4
    count = units // CHUNK

    def kernel(pos_ref, mask_ref, *refs):
        parts, (x_ref, out, lhs, rhs, result, sems) = refs[: len(pieces)], refs[len(pieces) :]
        for k in range(4):
            rhs[k * size : (k + 1) * size] = token_rows(pos_ref, x_ref, k)
        gather_rows(parts, lhs)
        copies = []
        for i in range(count):
            full = lax.dot_general(
                lhs[:, i * CHUNK : (i + 1) * CHUNK], rhs[...], dims(0, 0), preferred_element_type=F32
            )
            chunk_of(result, i, True)[...] = masked(full, mask_ref, i * (CHUNK // BLOCK), 0).astype(BF16)
            copies.append(pltpu.make_async_copy(chunk_of(result, i, True), chunk_of(out, i, True), sems.at[i]))
            copies[-1].start()
        for copy in copies:
            copy.wait()

    return call(
        kernel, [SMEM, SMEM] + [VMEM] * len(pieces) + [VMEM], HBM,
        jax.ShapeDtypeStruct((units, width), BF16),
        [pltpu.VMEM((tokens, units), BF16), pltpu.VMEM((tokens, width), BF16), pltpu.VMEM((units, width), BF16),
         pltpu.SemaphoreType.DMA((count,))],
    )(pos, mask, *pieces, x)


def y_joined(pos, pieces):
    size, width = pieces[0].shape

    def kernel(pos_ref, *refs):
        for k in range(4):
            at = pl.multiple_of((pos_ref[1] + k) % 4 * size, size)
            refs[4][pl.ds(at, size), :] = refs[k][...]

    return call(kernel, [SMEM] + [VMEM] * 4, VMEM, jax.ShapeDtypeStruct((4 * size, width), BF16))(pos, *pieces)


def all_rows(pos, mine, other):
    half, width = mine.shape
    size = half // 2

    def kernel(pos_ref, mine_ref, other_ref, out):
        z, core = pos_ref[0], pos_ref[2]
        for k in range(2):
            here = pl.multiple_of((z + 2 * core + k) % 4 * size, size)
            there = pl.multiple_of((z + 2 * (1 - core) + k) % 4 * size, size)
            out[pl.ds(here, size), :] = mine_ref[k * size : (k + 1) * size]
            out[pl.ds(there, size), :] = other_ref[k * size : (k + 1) * size]

    return call(kernel, [SMEM, VMEM, VMEM], VMEM, jax.ShapeDtypeStruct((2 * half, width), BF16))(pos, mine, other)


def col_reduce(pos, kept, sent):
    mine = kept + col_send(sent, CORE_SWAP).astype(F32)
    own, nxt, far, prv = jnp.split(mine, 4, axis=0)
    a = col_send(far.astype(BF16), y_step(2))
    b = col_send(nxt.astype(BF16), y_step(1))
    c = col_send(prv.astype(BF16), y_step(-1))
    own = (own + a.astype(F32) + b.astype(F32) + c.astype(F32)).astype(BF16)
    own = (own.astype(F32) + col_send(own, H_SWAP).astype(F32)).astype(BF16)
    far = col_send(own, y_step(2))
    prv = col_send(own, y_step(1))
    nxt = col_send(own, y_step(-1))
    mine = y_joined(pos, (own, nxt, far, prv))
    return all_rows(pos, mine, col_send(mine, CORE_SWAP))


def activate(value):
    return jax.nn.gelu(value, approximate=True)


def activated(part, arrived):
    def kernel(part_ref, arrived_ref, active, slope):
        value, pull_back = jax.vjp(activate, part_ref[...] + arrived_ref[...].astype(F32))
        active[...] = value.astype(BF16)
        slope[...] = pull_back(jnp.ones_like(value))[0]

    return call(
        kernel, [VMEM] * 2, [VMEM] * 2,
        [jax.ShapeDtypeStruct(part.shape, BF16), jax.ShapeDtypeStruct(part.shape, F32)],
    )(part, arrived)


def body(inputs, up_weight, down_weight, up_mask, down_mask, cotangent):
    col = lax.axis_index("col")
    pos = jnp.stack([lax.axis_index("row") % 4, col // 2 % 4, col % 2]).astype(jnp.int32)
    hidden = z_reduce(split_part(pos, up_mask, inputs, up_weight, False))
    active_own, slope = activated(hidden, x_swap(hidden))
    active = z_collect(active_own)
    grad = z_reduce(split_part(pos, down_mask, cotangent, down_weight, True))
    hidden_grad = z_collect(((grad + x_swap(grad).astype(F32)) * slope).astype(BF16))
    output = col_reduce(pos, *down_part(pos, down_mask, active, down_weight, False))
    input_grad = col_reduce(pos, *down_part(pos, up_mask, hidden_grad, up_weight, True))
    down_grad = down_gradient(pos, down_mask, active, cotangent)
    up_grad = up_gradient(pos, up_mask, inputs, hidden_grad)
    return (output, input_grad, up_grad, down_grad)


def solution(mesh):
    in_specs = (
        P(None, "row"),
        P("row", "col"),
        P("col", "row"),
        P("row", "col"),
        P("col", "row"),
        P(None, "row"),
    )
    out_specs = (P(None, "row"), P(None, "row"), P("row", "col"), P("col", "row"))
    return jax.shard_map(body, mesh=mesh, in_specs=in_specs, out_specs=out_specs, check_vma=False)
```

```python
import jax
import jax.numpy as jnp
from jax import lax
from jax.experimental import pallas as pl
from jax.experimental.pallas import tpu as pltpu
from jax.sharding import PartitionSpec as P


F32 = jnp.float32
BF16 = jnp.bfloat16
BLOCK = 128


def z_step(d):
    return [(x * 4 + z, x * 4 + (z + d) % 4) for x in range(2) for z in range(4)]


def y_step(d):
    return [(h * 8 + y * 2 + c, h * 8 + (y + d) % 4 * 2 + c) for h in range(2) for y in range(4) for c in range(2)]


X_SWAP = [(i, i ^ 4) for i in range(8)]
CORE_SWAP = [(i, i ^ 1) for i in range(16)]
H_SWAP = [(i, i ^ 8) for i in range(16)]


def row_send(v, perm):
    return lax.ppermute(v, "row", perm)


def col_send(v, perm):
    return lax.ppermute(v, "col", perm)


def masked(w, mask_ref, row0, col0):
    rows = []
    for r in range(w.shape[0] // BLOCK):
        row = w[r * BLOCK : (r + 1) * BLOCK]
        cols = []
        for c in range(w.shape[1] // BLOCK):
            piece = row[:, c * BLOCK : (c + 1) * BLOCK]
            cols.append(jnp.where(mask_ref[row0 + r, col0 + c] > 0, piece, jnp.zeros_like(piece)))
        rows.append(jnp.concatenate(cols, axis=1))
    return jnp.concatenate(rows, axis=0)


def dims(lhs, rhs):
    return (((lhs,), (rhs,)), ((), ()))


VMEM = pl.BlockSpec(memory_space=pltpu.VMEM)
SMEM = pl.BlockSpec(memory_space=pltpu.SMEM)
HBM = pl.BlockSpec(memory_space=pl.ANY)
CHUNK = 256


def call(body, in_specs, out_specs, out_shape, scratch=()):
    return pl.pallas_call(
        body,
        in_specs=in_specs,
        out_specs=out_specs,
        out_shape=out_shape,
        scratch_shapes=scratch,
        compiler_params=pltpu.CompilerParams(vmem_limit_bytes=50 * 1024 * 1024),
    )


def chunk_of(ref, i, rows):
    at = pl.ds(i * CHUNK, CHUNK)
    return ref.at[at, :] if rows else ref.at[:, at]


def spans(size, widths):
    at = 0
    for width in widths:
        width = min(width, size - at)
        if width:
            yield at, width
        at += width
    if at < size:
        yield at, size - at


def span_of(ref, span, rows):
    return ref.at[pl.ds(*span), :] if rows else ref.at[:, pl.ds(*span)]


def times_span(lhs, w, mask_ref, span, rows):
    first = span[0] // BLOCK
    tile = masked(span_of(w, span, rows)[...], mask_ref, *((first, 0) if rows else (0, first)))
    return lax.dot_general(lhs, tile, dims(1, 1 if rows else 0), preferred_element_type=F32)


def split_part(pos, mask, x, w, transposed):
    units = w.shape[0] if transposed else w.shape[1]
    tokens = x.shape[0] // 4
    half = tokens // 2
    parts = list(spans(units, (896, 896) if transposed else (512, 512)))
    count = 0 if transposed else len(parts)

    def kernel(pos_ref, mask_ref, x_hbm, w_in, far_a, far_b, own, nxt, prv, x_ref, w_ref, sems):
        z = pos_ref[0]
        x_copies = []
        for k in range(4):
            at = pl.multiple_of((z + k) % 4 * tokens, tokens)
            to = pl.ds(k * tokens, tokens)
            x_copies.append(pltpu.make_async_copy(x_hbm.at[pl.ds(at, tokens), :], x_ref.at[to, :], sems.at[count + k]))
            x_copies[-1].start()
        copies = [
            pltpu.make_async_copy(span_of(w_in, s, False), span_of(w_ref, s, False), sems.at[i])
            for i, s in enumerate(parts[:count])
        ]
        for copy in copies:
            copy.start()
        for copy in x_copies:
            copy.wait()
        for i, span in enumerate(parts):
            if not transposed:
                copies[i].wait()
            part = times_span(x_ref[...], w_in if transposed else w_ref, mask_ref, span, transposed)
            at = pl.ds(*span)
            own[:, at] = part[:tokens]
            nxt[:, at] = part[tokens : 2 * tokens]
            far = part[2 * tokens : 3 * tokens].astype(BF16)
            far_a[:, at] = far[:half]
            far_b[:, at] = far[half:]
            prv[:, at] = part[3 * tokens :]

    shapes = [jax.ShapeDtypeStruct((half, units), BF16)] * 2 + [jax.ShapeDtypeStruct((tokens, units), F32)] * 3
    return call(
        kernel, [SMEM, SMEM, HBM, VMEM if transposed else HBM],
        [VMEM] * 5, shapes,
        [pltpu.VMEM(x.shape, BF16), pltpu.VMEM((16, 128) if transposed else w.shape, BF16),
         pltpu.SemaphoreType.DMA((count + 4,))],
    )(pos, mask, x, w)


def joined(nxt, prv, from_prv, from_nxt):
    tokens, units = nxt.shape
    half = tokens // 2

    def kernel(nxt_ref, prv_ref, a_ref, b_ref, up, down):
        up[:half] = (nxt_ref[:half] + a_ref[...].astype(F32)).astype(BF16)
        up[half:] = nxt_ref[half:].astype(BF16)
        down[:half] = prv_ref[:half].astype(BF16)
        down[half:] = (prv_ref[half:] + b_ref[...].astype(F32)).astype(BF16)

    return call(
        kernel, [VMEM] * 4, [VMEM] * 2, [jax.ShapeDtypeStruct((tokens, units), BF16)] * 2
    )(nxt, prv, from_prv, from_nxt)


def z_reduce(pieces):
    far_a, far_b, own, nxt, prv = pieces
    from_prv = row_send(far_a, z_step(1))
    from_nxt = row_send(far_b, z_step(-1))
    up, down = joined(nxt, prv, from_prv, from_nxt)
    a = row_send(up, z_step(1))
    b = row_send(down, z_step(-1))
    return own + a.astype(F32) + b.astype(F32)


def x_swap(part):
    return row_send(part.astype(BF16), X_SWAP)


def z_collect(own):
    half = own.shape[0] // 2
    prv = row_send(own, z_step(1))
    nxt = row_send(own, z_step(-1))
    far_a = row_send(nxt[:half], z_step(-1))
    far_b = row_send(prv[half:], z_step(1))
    return own, nxt, far_a, far_b, prv


def gather_rows(refs, scratch):
    at = 0
    for ref in refs:
        scratch[at : at + ref.shape[0]] = ref[...]
        at += ref.shape[0]


def down_part(pos, mask, pieces, w, transposed):
    width = w.shape[0] if transposed else w.shape[1]
    units = w.shape[1] if transposed else w.shape[0]
    tokens = sum(p.shape[0] for p in pieces)
    half, size = tokens // 2, tokens // 8

    def kernel(pos_ref, mask_ref, *refs):
        parts, (w_ref, kept, sent, lhs) = refs[: len(pieces)], refs[len(pieces) :]
        y, core = pos_ref[1], pos_ref[2]
        block = 0
        for part in parts:
            for at in range(0, part.shape[0], size):
                side = core if block < 4 else 1 - core
                to = pl.multiple_of(side * half + (block + 4 - y) % 4 * size, size)
                lhs[pl.ds(to, size), :] = part[at : at + size, :]
                block += 1
        for span in spans(width, (512, 512)):
            full = times_span(lhs[...], w_ref, mask_ref, span, transposed)
            kept[:, pl.ds(*span)] = full[:half]
            sent[:, pl.ds(*span)] = full[half:].astype(BF16)

    return call(
        kernel, [SMEM, SMEM] + [VMEM] * (len(pieces) + 1), [VMEM] * 2,
        [jax.ShapeDtypeStruct((half, width), F32), jax.ShapeDtypeStruct((half, width), BF16)],
        [pltpu.VMEM((tokens, units), BF16)],
    )(pos, mask, *pieces, w)


def token_rows(pos_ref, x_ref, k):
    size = x_ref.shape[0] // 4
    return x_ref[pl.ds(pl.multiple_of((pos_ref[0] + k) % 4 * size, size), size), :]


def up_gradient(pos, mask, x, pieces):
    tokens, width = x.shape
    units = pieces[0].shape[1]
    size = tokens // 4
    count = units // CHUNK

    def kernel(pos_ref, mask_ref, x_ref, *refs):
        parts, (out, lhs, rhs, result, sems) = refs[: len(pieces)], refs[len(pieces) :]
        for k in range(4):
            lhs[:, k * size : (k + 1) * size] = token_rows(pos_ref, x_ref, k).T
        gather_rows(parts, rhs)
        copies = []
        for i in range(count):
            full = lax.dot_general(
                lhs[...], rhs[:, i * CHUNK : (i + 1) * CHUNK], dims(1, 0), preferred_element_type=F32
            )
            chunk_of(result, i, False)[...] = masked(full, mask_ref, 0, i * (CHUNK // BLOCK)).astype(BF16)
            copies.append(pltpu.make_async_copy(chunk_of(result, i, False), chunk_of(out, i, False), sems.at[i]))
            copies[-1].start()
        for copy in copies:
            copy.wait()

    return call(
        kernel, [SMEM, SMEM, VMEM] + [VMEM] * len(pieces), HBM, jax.ShapeDtypeStruct((width, units), BF16),
        [pltpu.VMEM((width, tokens), BF16), pltpu.VMEM((tokens, units), BF16), pltpu.VMEM((width, units), BF16),
         pltpu.SemaphoreType.DMA((count,))],
    )(pos, mask, x, *pieces)


def down_gradient(pos, mask, pieces, x):
    tokens, width = x.shape
    units = pieces[0].shape[1]
    size = tokens // 4
    count = units // CHUNK

    def kernel(pos_ref, mask_ref, *refs):
        parts, (x_ref, out, lhs, rhs, result, sems) = refs[: len(pieces)], refs[len(pieces) :]
        for k in range(4):
            rhs[k * size : (k + 1) * size] = token_rows(pos_ref, x_ref, k)
        gather_rows(parts, lhs)
        copies = []
        for i in range(count):
            full = lax.dot_general(
                lhs[:, i * CHUNK : (i + 1) * CHUNK], rhs[...], dims(0, 0), preferred_element_type=F32
            )
            chunk_of(result, i, True)[...] = masked(full, mask_ref, i * (CHUNK // BLOCK), 0).astype(BF16)
            copies.append(pltpu.make_async_copy(chunk_of(result, i, True), chunk_of(out, i, True), sems.at[i]))
            copies[-1].start()
        for copy in copies:
            copy.wait()

    return call(
        kernel, [SMEM, SMEM] + [VMEM] * len(pieces) + [VMEM], HBM,
        jax.ShapeDtypeStruct((units, width), BF16),
        [pltpu.VMEM((tokens, units), BF16), pltpu.VMEM((tokens, width), BF16), pltpu.VMEM((units, width), BF16),
         pltpu.SemaphoreType.DMA((count,))],
    )(pos, mask, *pieces, x)


def y_joined(pos, pieces):
    size, width = pieces[0].shape

    def kernel(pos_ref, *refs):
        for k in range(4):
            at = pl.multiple_of((pos_ref[1] + k) % 4 * size, size)
            refs[4][pl.ds(at, size), :] = refs[k][...]

    return call(kernel, [SMEM] + [VMEM] * 4, VMEM, jax.ShapeDtypeStruct((4 * size, width), BF16))(pos, *pieces)


def all_rows(pos, mine, other):
    half, width = mine.shape
    size = half // 2

    def kernel(pos_ref, mine_ref, other_ref, out):
        z, core = pos_ref[0], pos_ref[2]
        for k in range(2):
            here = pl.multiple_of((z + 2 * core + k) % 4 * size, size)
            there = pl.multiple_of((z + 2 * (1 - core) + k) % 4 * size, size)
            out[pl.ds(here, size), :] = mine_ref[k * size : (k + 1) * size]
            out[pl.ds(there, size), :] = other_ref[k * size : (k + 1) * size]

    return call(kernel, [SMEM, VMEM, VMEM], VMEM, jax.ShapeDtypeStruct((2 * half, width), BF16))(pos, mine, other)


def col_reduce(pos, kept, sent):
    mine = kept + col_send(sent, CORE_SWAP).astype(F32)
    own, nxt, far, prv = jnp.split(mine, 4, axis=0)
    a = col_send(far.astype(BF16), y_step(2))
    b = col_send(nxt.astype(BF16), y_step(1))
    c = col_send(prv.astype(BF16), y_step(-1))
    own = (own + a.astype(F32) + b.astype(F32) + c.astype(F32)).astype(BF16)
    own = (own.astype(F32) + col_send(own, H_SWAP).astype(F32)).astype(BF16)
    far = col_send(own, y_step(2))
    prv = col_send(own, y_step(1))
    nxt = col_send(own, y_step(-1))
    mine = y_joined(pos, (own, nxt, far, prv))
    return all_rows(pos, mine, col_send(mine, CORE_SWAP))


def activate(value):
    return jax.nn.gelu(value, approximate=True)


def activated(part, arrived):
    def kernel(part_ref, arrived_ref, active, slope):
        value, pull_back = jax.vjp(activate, part_ref[...] + arrived_ref[...].astype(F32))
        active[...] = value.astype(BF16)
        slope[...] = pull_back(jnp.ones_like(value))[0]

    return call(
        kernel, [VMEM] * 2, [VMEM] * 2,
        [jax.ShapeDtypeStruct(part.shape, BF16), jax.ShapeDtypeStruct(part.shape, F32)],
    )(part, arrived)


def body(inputs, up_weight, down_weight, up_mask, down_mask, cotangent):
    col = lax.axis_index("col")
    pos = jnp.stack([lax.axis_index("row") % 4, col // 2 % 4, col % 2]).astype(jnp.int32)
    hidden = z_reduce(split_part(pos, up_mask, inputs, up_weight, False))
    active_own, slope = activated(hidden, x_swap(hidden))
    active = z_collect(active_own)
    grad = z_reduce(split_part(pos, down_mask, cotangent, down_weight, True))
    hidden_grad = z_collect(((grad + x_swap(grad).astype(F32)) * slope).astype(BF16))
    output = col_reduce(pos, *down_part(pos, down_mask, active, down_weight, False))
    input_grad = col_reduce(pos, *down_part(pos, up_mask, hidden_grad, up_weight, True))
    down_grad = down_gradient(pos, down_mask, active, cotangent)
    up_grad = up_gradient(pos, up_mask, inputs, hidden_grad)
    return (output, input_grad, up_grad, down_grad)


def solution(mesh):
    in_specs = (
        P(None, "row"),
        P("row", "col"),
        P("col", "row"),
        P("row", "col"),
        P("col", "row"),
        P(None, "row"),
    )
    out_specs = (P(None, "row"), P(None, "row"), P("row", "col"), P("col", "row"))
    return jax.shard_map(body, mesh=mesh, in_specs=in_specs, out_specs=out_specs, check_vma=False)
```

```python
import jax
import jax.numpy as jnp
from jax import lax
from jax.experimental import pallas as pl
from jax.experimental.pallas import tpu as pltpu
from jax.sharding import PartitionSpec as P


F32 = jnp.float32
BF16 = jnp.bfloat16
BLOCK = 128


def z_step(d):
    return [(x * 4 + z, x * 4 + (z + d) % 4) for x in range(2) for z in range(4)]


def y_step(d):
    return [(h * 8 + y * 2 + c, h * 8 + (y + d) % 4 * 2 + c) for h in range(2) for y in range(4) for c in range(2)]


X_SWAP = [(i, i ^ 4) for i in range(8)]
CORE_SWAP = [(i, i ^ 1) for i in range(16)]
H_SWAP = [(i, i ^ 8) for i in range(16)]
Y1_SWAP = [(i, i ^ 2) for i in range(16)]
Y3_SWAP = [(i, i ^ 6) for i in range(16)]


def row_send(v, perm):
    return lax.ppermute(v, "row", perm)


def col_send(v, perm):
    return lax.ppermute(v, "col", perm)


def masked(w, mask_ref, row0, col0):
    rows = []
    for r in range(w.shape[0] // BLOCK):
        row = w[r * BLOCK : (r + 1) * BLOCK]
        cols = []
        for c in range(w.shape[1] // BLOCK):
            piece = row[:, c * BLOCK : (c + 1) * BLOCK]
            cols.append(jnp.where(mask_ref[row0 + r, col0 + c] > 0, piece, jnp.zeros_like(piece)))
        rows.append(jnp.concatenate(cols, axis=1))
    return jnp.concatenate(rows, axis=0)


def dims(lhs, rhs):
    return (((lhs,), (rhs,)), ((), ()))


VMEM = pl.BlockSpec(memory_space=pltpu.VMEM)
SMEM = pl.BlockSpec(memory_space=pltpu.SMEM)
HBM = pl.BlockSpec(memory_space=pl.ANY)
CHUNK = 256


def call(body, in_specs, out_specs, out_shape, scratch=()):
    return pl.pallas_call(
        body,
        in_specs=in_specs,
        out_specs=out_specs,
        out_shape=out_shape,
        scratch_shapes=scratch,
        compiler_params=pltpu.CompilerParams(vmem_limit_bytes=50 * 1024 * 1024),
    )


def chunk_of(ref, i, rows):
    at = pl.ds(i * CHUNK, CHUNK)
    return ref.at[at, :] if rows else ref.at[:, at]


def spans(size, widths):
    at = 0
    for width in widths:
        width = min(width, size - at)
        if width:
            yield at, width
        at += width
    if at < size:
        yield at, size - at


def span_of(ref, span, rows):
    return ref.at[pl.ds(*span), :] if rows else ref.at[:, pl.ds(*span)]


def times_span(lhs, w, mask_ref, span, rows):
    first = span[0] // BLOCK
    tile = masked(span_of(w, span, rows)[...], mask_ref, *((first, 0) if rows else (0, first)))
    return lax.dot_general(lhs, tile, dims(1, 1 if rows else 0), preferred_element_type=F32)


def split_part(pos, mask, x, w, transposed):
    units = w.shape[0] if transposed else w.shape[1]
    tokens = x.shape[0] // 4
    half = tokens // 2
    parts = list(spans(units, (896, 896) if transposed else (512, 512)))
    count = 0 if transposed else len(parts)

    def kernel(pos_ref, mask_ref, x_hbm, w_in, far_a, far_b, own, nxt, prv, x_ref, w_ref, sems):
        z = pos_ref[0]
        x_copies = []
        for k in range(4):
            at = pl.multiple_of((z + k) % 4 * tokens, tokens)
            to = pl.ds(k * tokens, tokens)
            x_copies.append(pltpu.make_async_copy(x_hbm.at[pl.ds(at, tokens), :], x_ref.at[to, :], sems.at[count + k]))
            x_copies[-1].start()
        copies = [
            pltpu.make_async_copy(span_of(w_in, s, False), span_of(w_ref, s, False), sems.at[i])
            for i, s in enumerate(parts[:count])
        ]
        for copy in copies:
            copy.start()
        for copy in x_copies:
            copy.wait()
        for i, span in enumerate(parts):
            if not transposed:
                copies[i].wait()
            part = times_span(x_ref[...], w_in if transposed else w_ref, mask_ref, span, transposed)
            at = pl.ds(*span)
            own[:, at] = part[:tokens]
            nxt[:, at] = part[tokens : 2 * tokens]
            far = part[2 * tokens : 3 * tokens].astype(BF16)
            far_a[:, at] = far[:half]
            far_b[:, at] = far[half:]
            prv[:, at] = part[3 * tokens :]

    shapes = [jax.ShapeDtypeStruct((half, units), BF16)] * 2 + [jax.ShapeDtypeStruct((tokens, units), F32)] * 3
    return call(
        kernel, [SMEM, SMEM, HBM, VMEM if transposed else HBM],
        [VMEM] * 5, shapes,
        [pltpu.VMEM(x.shape, BF16), pltpu.VMEM((16, 128) if transposed else w.shape, BF16),
         pltpu.SemaphoreType.DMA((count + 4,))],
    )(pos, mask, x, w)


def joined(nxt, prv, from_prv, from_nxt):
    tokens, units = nxt.shape
    half = tokens // 2

    def kernel(nxt_ref, prv_ref, a_ref, b_ref, up, down):
        up[:half] = (nxt_ref[:half] + a_ref[...].astype(F32)).astype(BF16)
        up[half:] = nxt_ref[half:].astype(BF16)
        down[:half] = prv_ref[:half].astype(BF16)
        down[half:] = (prv_ref[half:] + b_ref[...].astype(F32)).astype(BF16)

    return call(
        kernel, [VMEM] * 4, [VMEM] * 2, [jax.ShapeDtypeStruct((tokens, units), BF16)] * 2
    )(nxt, prv, from_prv, from_nxt)


def z_reduce(pieces):
    far_a, far_b, own, nxt, prv = pieces
    from_prv = row_send(far_a, z_step(1))
    from_nxt = row_send(far_b, z_step(-1))
    up, down = joined(nxt, prv, from_prv, from_nxt)
    a = row_send(up, z_step(1))
    b = row_send(down, z_step(-1))
    return own + a.astype(F32) + b.astype(F32)


def x_swap(part):
    return row_send(part.astype(BF16), X_SWAP)


def z_collect(own):
    half = own.shape[0] // 2
    prv = row_send(own, z_step(1))
    nxt = row_send(own, z_step(-1))
    far_a = row_send(nxt[:half], z_step(-1))
    far_b = row_send(prv[half:], z_step(1))
    return own, nxt, far_a, far_b, prv


def gather_rows(refs, scratch):
    at = 0
    for ref in refs:
        scratch[at : at + ref.shape[0]] = ref[...]
        at += ref.shape[0]


def ring_place(y, block):
    return (block + 4 - y) % 4


def swap_place(y, block):
    apart = y ^ block
    return jnp.where(apart == 0, 0, apart % 3 + 1)


def down_part(pos, mask, pieces, w, transposed, place):
    width = w.shape[0] if transposed else w.shape[1]
    units = w.shape[1] if transposed else w.shape[0]
    tokens = sum(p.shape[0] for p in pieces)
    half, size = tokens // 2, tokens // 8

    def kernel(pos_ref, mask_ref, *refs):
        parts, (w_ref, kept, sent, lhs) = refs[: len(pieces)], refs[len(pieces) :]
        y, core = pos_ref[1], pos_ref[2]
        block = 0
        for part in parts:
            for at in range(0, part.shape[0], size):
                side = core if block < 4 else 1 - core
                to = pl.multiple_of(side * half + place(y, block % 4) * size, size)
                lhs[pl.ds(to, size), :] = part[at : at + size, :]
                block += 1
        for span in spans(width, (512, 512)):
            full = times_span(lhs[...], w_ref, mask_ref, span, transposed)
            kept[:, pl.ds(*span)] = full[:half]
            sent[:, pl.ds(*span)] = full[half:].astype(BF16)

    return call(
        kernel, [SMEM, SMEM] + [VMEM] * (len(pieces) + 1), [VMEM] * 2,
        [jax.ShapeDtypeStruct((half, width), F32), jax.ShapeDtypeStruct((half, width), BF16)],
        [pltpu.VMEM((tokens, units), BF16)],
    )(pos, mask, *pieces, w)


def token_rows(pos_ref, x_ref, k):
    size = x_ref.shape[0] // 4
    return x_ref[pl.ds(pl.multiple_of((pos_ref[0] + k) % 4 * size, size), size), :]


def up_gradient(pos, mask, x, pieces):
    tokens, width = x.shape
    units = pieces[0].shape[1]
    size = tokens // 4
    count = units // CHUNK

    def kernel(pos_ref, mask_ref, x_ref, *refs):
        parts, (out, lhs, rhs, result, sems) = refs[: len(pieces)], refs[len(pieces) :]
        for k in range(4):
            lhs[:, k * size : (k + 1) * size] = token_rows(pos_ref, x_ref, k).T
        gather_rows(parts, rhs)
        copies = []
        for i in range(count):
            full = lax.dot_general(
                lhs[...], rhs[:, i * CHUNK : (i + 1) * CHUNK], dims(1, 0), preferred_element_type=F32
            )
            chunk_of(result, i, False)[...] = masked(full, mask_ref, 0, i * (CHUNK // BLOCK)).astype(BF16)
            copies.append(pltpu.make_async_copy(chunk_of(result, i, False), chunk_of(out, i, False), sems.at[i]))
            copies[-1].start()
        for copy in copies:
            copy.wait()

    return call(
        kernel, [SMEM, SMEM, VMEM] + [VMEM] * len(pieces), HBM, jax.ShapeDtypeStruct((width, units), BF16),
        [pltpu.VMEM((width, tokens), BF16), pltpu.VMEM((tokens, units), BF16), pltpu.VMEM((width, units), BF16),
         pltpu.SemaphoreType.DMA((count,))],
    )(pos, mask, x, *pieces)


def down_gradient(pos, mask, pieces, x):
    tokens, width = x.shape
    units = pieces[0].shape[1]
    size = tokens // 4
    count = units // CHUNK

    def kernel(pos_ref, mask_ref, *refs):
        parts, (x_ref, out, lhs, rhs, result, sems) = refs[: len(pieces)], refs[len(pieces) :]
        for k in range(4):
            rhs[k * size : (k + 1) * size] = token_rows(pos_ref, x_ref, k)
        gather_rows(parts, lhs)
        copies = []
        for i in range(count):
            full = lax.dot_general(
                lhs[:, i * CHUNK : (i + 1) * CHUNK], rhs[...], dims(0, 0), preferred_element_type=F32
            )
            chunk_of(result, i, True)[...] = masked(full, mask_ref, i * (CHUNK // BLOCK), 0).astype(BF16)
            copies.append(pltpu.make_async_copy(chunk_of(result, i, True), chunk_of(out, i, True), sems.at[i]))
            copies[-1].start()
        for copy in copies:
            copy.wait()

    return call(
        kernel, [SMEM, SMEM] + [VMEM] * len(pieces) + [VMEM], HBM,
        jax.ShapeDtypeStruct((units, width), BF16),
        [pltpu.VMEM((tokens, units), BF16), pltpu.VMEM((tokens, width), BF16), pltpu.VMEM((units, width), BF16),
         pltpu.SemaphoreType.DMA((count,))],
    )(pos, mask, *pieces, x)


def y_joined(pos, pieces, place):
    width = pieces[0].shape[1]
    rows = sum(p.shape[0] for p in pieces)
    size = rows // 4

    def kernel(pos_ref, *refs):
        parts, out = refs[:-1], refs[-1]
        y = pos_ref[1]
        blocks = [(part, at) for part in parts for at in range(0, part.shape[0], size)]
        for k, (part, at) in enumerate(blocks):
            to = pl.multiple_of(place(y, k) * size, size)
            out[pl.ds(to, size), :] = part[at : at + size, :]

    return call(kernel, [SMEM] + [VMEM] * len(pieces), VMEM, jax.ShapeDtypeStruct((rows, width), BF16))(pos, *pieces)


def all_rows(pos, mine, other):
    half, width = mine.shape
    size = half // 2

    def kernel(pos_ref, mine_ref, other_ref, out):
        z, core = pos_ref[0], pos_ref[2]
        for k in range(2):
            here = pl.multiple_of((z + 2 * core + k) % 4 * size, size)
            there = pl.multiple_of((z + 2 * (1 - core) + k) % 4 * size, size)
            out[pl.ds(here, size), :] = mine_ref[k * size : (k + 1) * size]
            out[pl.ds(there, size), :] = other_ref[k * size : (k + 1) * size]

    return call(kernel, [SMEM, VMEM, VMEM], VMEM, jax.ShapeDtypeStruct((2 * half, width), BF16))(pos, mine, other)


def col_reduce(pos, kept, sent):
    mine = kept + col_send(sent, CORE_SWAP).astype(F32)
    own, nxt, far, prv = jnp.split(mine, 4, axis=0)
    a = col_send(far.astype(BF16), y_step(2))
    b = col_send(nxt.astype(BF16), y_step(1))
    c = col_send(prv.astype(BF16), y_step(-1))
    own = (own + a.astype(F32) + b.astype(F32) + c.astype(F32)).astype(BF16)
    own = (own.astype(F32) + col_send(own, H_SWAP).astype(F32)).astype(BF16)
    far = col_send(own, y_step(2))
    prv = col_send(own, y_step(1))
    nxt = col_send(own, y_step(-1))
    mine = y_joined(pos, (own, nxt, far, prv), lambda y, k: (y + k) % 4)
    return all_rows(pos, mine, col_send(mine, CORE_SWAP))


def col_reduce_by_swaps(pos, kept, sent):
    mine = kept + col_send(sent, CORE_SWAP).astype(F32)
    half, quarter = mine.shape[0] // 2, mine.shape[0] // 4
    mine = mine[:half] + col_send(mine[half:].astype(BF16), Y1_SWAP).astype(F32)
    own = mine[:quarter] + col_send(mine[quarter:].astype(BF16), Y3_SWAP).astype(F32)
    own = own.astype(BF16)
    own = (own.astype(F32) + col_send(own, H_SWAP).astype(F32)).astype(BF16)
    pair = jnp.concatenate([own, col_send(own, Y3_SWAP)], axis=0)
    mine = y_joined(pos, (pair, col_send(pair, Y1_SWAP)), lambda y, k: y ^ (0, 3, 1, 2)[k])
    return all_rows(pos, mine, col_send(mine, CORE_SWAP))


def activate(value):
    return jax.nn.gelu(value, approximate=True)


def activated(part, arrived):
    def kernel(part_ref, arrived_ref, active, slope):
        value, pull_back = jax.vjp(activate, part_ref[...] + arrived_ref[...].astype(F32))
        active[...] = value.astype(BF16)
        slope[...] = pull_back(jnp.ones_like(value))[0]

    return call(
        kernel, [VMEM] * 2, [VMEM] * 2,
        [jax.ShapeDtypeStruct(part.shape, BF16), jax.ShapeDtypeStruct(part.shape, F32)],
    )(part, arrived)


def body(inputs, up_weight, down_weight, up_mask, down_mask, cotangent):
    col = lax.axis_index("col")
    pos = jnp.stack([lax.axis_index("row") % 4, col // 2 % 4, col % 2]).astype(jnp.int32)
    hidden = z_reduce(split_part(pos, up_mask, inputs, up_weight, False))
    active_own, slope = activated(hidden, x_swap(hidden))
    active = z_collect(active_own)
    grad = z_reduce(split_part(pos, down_mask, cotangent, down_weight, True))
    hidden_grad = z_collect(((grad + x_swap(grad).astype(F32)) * slope).astype(BF16))
    output = col_reduce_by_swaps(pos, *down_part(pos, down_mask, active, down_weight, False, swap_place))
    input_grad = col_reduce(pos, *down_part(pos, up_mask, hidden_grad, up_weight, True, ring_place))
    down_grad = down_gradient(pos, down_mask, active, cotangent)
    up_grad = up_gradient(pos, up_mask, inputs, hidden_grad)
    return (output, input_grad, up_grad, down_grad)


def solution(mesh):
    in_specs = (
        P(None, "row"),
        P("row", "col"),
        P("col", "row"),
        P("row", "col"),
        P("col", "row"),
        P(None, "row"),
    )
    out_specs = (P(None, "row"), P(None, "row"), P("row", "col"), P("col", "row"))
    return jax.shard_map(body, mesh=mesh, in_specs=in_specs, out_specs=out_specs, check_vma=False)
```

```python
import jax
import jax.numpy as jnp
from jax import lax
from jax.experimental import pallas as pl
from jax.experimental.pallas import tpu as pltpu
from jax.sharding import PartitionSpec as P


F32 = jnp.float32
BF16 = jnp.bfloat16
BLOCK = 128


def z_step(d):
    return [(x * 4 + z, x * 4 + (z + d) % 4) for x in range(2) for z in range(4)]


def y_step(d):
    return [(h * 8 + y * 2 + c, h * 8 + (y + d) % 4 * 2 + c) for h in range(2) for y in range(4) for c in range(2)]


X_SWAP = [(i, i ^ 4) for i in range(8)]
CORE_SWAP = [(i, i ^ 1) for i in range(16)]
H_SWAP = [(i, i ^ 8) for i in range(16)]


def row_send(v, perm):
    return lax.ppermute(v, "row", perm)


def col_send(v, perm):
    return lax.ppermute(v, "col", perm)


def masked(w, mask_ref, row0, col0):
    rows = []
    for r in range(w.shape[0] // BLOCK):
        row = w[r * BLOCK : (r + 1) * BLOCK]
        cols = []
        for c in range(w.shape[1] // BLOCK):
            piece = row[:, c * BLOCK : (c + 1) * BLOCK]
            cols.append(jnp.where(mask_ref[row0 + r, col0 + c] > 0, piece, jnp.zeros_like(piece)))
        rows.append(jnp.concatenate(cols, axis=1))
    return jnp.concatenate(rows, axis=0)


def dims(lhs, rhs):
    return (((lhs,), (rhs,)), ((), ()))


VMEM = pl.BlockSpec(memory_space=pltpu.VMEM)
SMEM = pl.BlockSpec(memory_space=pltpu.SMEM)
HBM = pl.BlockSpec(memory_space=pltpu.HBM)
CHUNK = 256


def call(body, in_specs, out_specs, out_shape, scratch=()):
    return pl.pallas_call(
        body,
        in_specs=in_specs,
        out_specs=out_specs,
        out_shape=out_shape,
        scratch_shapes=scratch,
        compiler_params=pltpu.CompilerParams(vmem_limit_bytes=20 * 1024 * 1024),
    )


def chunk_of(ref, i, rows):
    at = pl.ds(i * CHUNK, CHUNK)
    return ref.at[at, :] if rows else ref.at[:, at]


def spans(size, widths):
    at = 0
    for width in widths:
        width = min(width, size - at)
        if width:
            yield at, width
        at += width
    if at < size:
        yield at, size - at


def span_of(ref, span, rows):
    return ref.at[pl.ds(*span), :] if rows else ref.at[:, pl.ds(*span)]


def times_span(lhs, w, mask_ref, span, rows, kept):
    first = span[0] // BLOCK
    tile = masked(span_of(w, span, rows)[...], mask_ref, *((first, 0) if rows else (0, first)))
    span_of(kept, span, rows)[...] = tile
    return lax.dot_general(lhs, tile, dims(1, 1 if rows else 0), preferred_element_type=F32)


def row_fetches(z, x_hbm, x_ref, sems, blocks):
    tokens = x_hbm.shape[0] // 4
    copies = []
    for i, k in enumerate(blocks):
        at = pl.multiple_of((z + k) % 4 * tokens, tokens)
        to = pl.ds(i * tokens, tokens)
        copies.append(pltpu.make_async_copy(x_hbm.at[pl.ds(at, tokens), :], x_ref.at[to, :], sems.at[i]))
    return copies


def hidden_far(pos, mask, x, w):
    units = w.shape[1]
    tokens = x.shape[0] // 4
    half = tokens // 2
    parts = list(spans(units, (256, 512, 512)))

    def kernel(pos_ref, mask_ref, x_hbm, w_hbm, far_a, far_b, kept, x_ref, w_ref, x_sems, sems):
        x_copies = row_fetches(pos_ref[0], x_hbm, x_ref, x_sems, (2,))
        copies = [
            pltpu.make_async_copy(span_of(w_hbm, s, False), span_of(w_ref, s, False), sems.at[i])
            for i, s in enumerate(parts)
        ]
        for copy in x_copies + copies:
            copy.start()
        x_copies[0].wait()
        for copy, span in zip(copies, parts):
            copy.wait()
            far = times_span(x_ref[...], w_ref, mask_ref, span, False, kept).astype(BF16)
            far_a[:, pl.ds(*span)] = far[:half]
            far_b[:, pl.ds(*span)] = far[half:]

    return call(
        kernel, [SMEM, SMEM, HBM, HBM], [VMEM] * 3,
        [jax.ShapeDtypeStruct((half, units), BF16)] * 2 + [jax.ShapeDtypeStruct(w.shape, BF16)],
        [pltpu.VMEM((tokens, x.shape[1]), BF16), pltpu.VMEM(w.shape, BF16), pltpu.SemaphoreType.DMA((1,)),
         pltpu.SemaphoreType.DMA((len(parts),))],
    )(pos, mask, x, w)


def hidden_near(pos, x, w):
    units = w.shape[1]
    tokens = x.shape[0] // 4

    def kernel(pos_ref, x_hbm, w_ref, own, nxt, prv, x_ref, x_sems):
        x_copies = row_fetches(pos_ref[0], x_hbm, x_ref, x_sems, (0, 1, 3))
        for copy in x_copies:
            copy.start()
        for copy in x_copies:
            copy.wait()
        for span in spans(units, (896, 896)):
            at = pl.ds(*span)
            part = lax.dot_general(x_ref[...], w_ref[:, at], dims(1, 0), preferred_element_type=F32)
            own[:, at] = part[:tokens]
            nxt[:, at] = part[tokens : 2 * tokens]
            prv[:, at] = part[2 * tokens :]

    return call(
        kernel, [SMEM, HBM, VMEM], [VMEM] * 3, [jax.ShapeDtypeStruct((tokens, units), F32)] * 3,
        [pltpu.VMEM((3 * tokens, x.shape[1]), BF16), pltpu.SemaphoreType.DMA((3,))],
    )(pos, x, w)


def grad_part(pos, mask, x, w):
    units = w.shape[0]
    tokens = x.shape[0] // 4
    half = tokens // 2
    parts = list(spans(units, (512, 512, 768)))

    def kernel(pos_ref, mask_ref, x_hbm, w_hbm, far_a, far_b, own, nxt, prv, kept, x_ref, w_ref, x_sems, sems):
        x_copies = row_fetches(pos_ref[0], x_hbm, x_ref, x_sems, (0, 1, 2, 3))
        copies = [
            pltpu.make_async_copy(span_of(w_hbm, s, True), span_of(w_ref, s, True), sems.at[i])
            for i, s in enumerate(parts)
        ]
        for copy in x_copies + copies:
            copy.start()
        for copy in x_copies:
            copy.wait()
        for copy, span in zip(copies, parts):
            copy.wait()
            at = pl.ds(*span)
            part = times_span(x_ref[...], w_ref, mask_ref, span, True, kept)
            own[:, at] = part[:tokens]
            nxt[:, at] = part[tokens : 2 * tokens]
            far = part[2 * tokens : 3 * tokens].astype(BF16)
            far_a[:, at] = far[:half]
            far_b[:, at] = far[half:]
            prv[:, at] = part[3 * tokens :]

    return call(
        kernel, [SMEM, SMEM, HBM, HBM], [VMEM] * 6,
        [jax.ShapeDtypeStruct((half, units), BF16)] * 2 + [jax.ShapeDtypeStruct((tokens, units), F32)] * 3
        + [jax.ShapeDtypeStruct(w.shape, BF16)],
        [pltpu.VMEM(x.shape, BF16), pltpu.VMEM(w.shape, BF16), pltpu.SemaphoreType.DMA((4,)),
         pltpu.SemaphoreType.DMA((len(parts),))],
    )(pos, mask, x, w)


def joined(nxt, prv, from_prv, from_nxt):
    tokens, units = nxt.shape
    half = tokens // 2

    def kernel(nxt_ref, prv_ref, a_ref, b_ref, up, down):
        up[:half] = (nxt_ref[:half] + a_ref[...].astype(F32)).astype(BF16)
        up[half:] = nxt_ref[half:].astype(BF16)
        down[:half] = prv_ref[:half].astype(BF16)
        down[half:] = (prv_ref[half:] + b_ref[...].astype(F32)).astype(BF16)

    return call(
        kernel, [VMEM] * 4, [VMEM] * 2, [jax.ShapeDtypeStruct((tokens, units), BF16)] * 2
    )(nxt, prv, from_prv, from_nxt)


def z_reduce(pieces):
    far_a, far_b, own, nxt, prv = pieces
    from_prv = row_send(far_a, z_step(1))
    from_nxt = row_send(far_b, z_step(-1))
    up, down = joined(nxt, prv, from_prv, from_nxt)
    a = row_send(up, z_step(1))
    b = row_send(down, z_step(-1))
    return own + a.astype(F32) + b.astype(F32)


def x_swap(part):
    return row_send(part.astype(BF16), X_SWAP)


def z_collect(own):
    half = own.shape[0] // 2
    prv = row_send(own, z_step(1))
    nxt = row_send(own, z_step(-1))
    far_a = row_send(nxt[:half], z_step(-1))
    far_b = row_send(prv[half:], z_step(1))
    return own, nxt, far_a, far_b, prv


def gather_rows(refs, scratch):
    at = 0
    for ref in refs:
        scratch[at : at + ref.shape[0]] = ref[...]
        at += ref.shape[0]


def down_part(pos, pieces, w, transposed):
    width = w.shape[0] if transposed else w.shape[1]
    units = w.shape[1] if transposed else w.shape[0]
    tokens = sum(p.shape[0] for p in pieces)
    half, size = tokens // 2, tokens // 8

    def kernel(pos_ref, *refs):
        parts, (w_ref, kept, sent, lhs) = refs[: len(pieces)], refs[len(pieces) :]
        y, core = pos_ref[1], pos_ref[2]
        block = 0
        for part in parts:
            for at in range(0, part.shape[0], size):
                side = core if block < 4 else 1 - core
                to = pl.multiple_of(side * half + (block + 4 - y) % 4 * size, size)
                lhs[pl.ds(to, size), :] = part[at : at + size, :]
                block += 1
        for span in spans(width, (512, 512)):
            full = lax.dot_general(
                lhs[...], span_of(w_ref, span, transposed)[...], dims(1, 1 if transposed else 0),
                preferred_element_type=F32,
            )
            kept[:, pl.ds(*span)] = full[:half]
            sent[:, pl.ds(*span)] = full[half:].astype(BF16)

    return call(
        kernel, [SMEM] + [VMEM] * (len(pieces) + 1), [VMEM] * 2,
        [jax.ShapeDtypeStruct((half, width), F32), jax.ShapeDtypeStruct((half, width), BF16)],
        [pltpu.VMEM((tokens, units), BF16)],
    )(pos, *pieces, w)


def token_rows(pos_ref, x_ref, k):
    size = x_ref.shape[0] // 4
    return x_ref[pl.ds(pl.multiple_of((pos_ref[0] + k) % 4 * size, size), size), :]


def up_gradient(pos, mask, x, pieces):
    tokens, width = x.shape
    units = pieces[0].shape[1]
    size = tokens // 4
    count = units // CHUNK

    def kernel(pos_ref, mask_ref, x_ref, *refs):
        parts, (out, lhs, rhs, result, sems) = refs[: len(pieces)], refs[len(pieces) :]
        for k in range(4):
            lhs[:, k * size : (k + 1) * size] = token_rows(pos_ref, x_ref, k).T
        gather_rows(parts, rhs)
        copies = []
        for i in range(count):
            full = lax.dot_general(
                lhs[...], rhs[:, i * CHUNK : (i + 1) * CHUNK], dims(1, 0), preferred_element_type=F32
            )
            chunk_of(result, i, False)[...] = masked(full, mask_ref, 0, i * (CHUNK // BLOCK)).astype(BF16)
            copies.append(pltpu.make_async_copy(chunk_of(result, i, False), chunk_of(out, i, False), sems.at[i]))
            copies[-1].start()
        for copy in copies:
            copy.wait()

    return call(
        kernel, [SMEM, SMEM, VMEM] + [VMEM] * len(pieces), HBM, jax.ShapeDtypeStruct((width, units), BF16),
        [pltpu.VMEM((width, tokens), BF16), pltpu.VMEM((tokens, units), BF16), pltpu.VMEM((width, units), BF16),
         pltpu.SemaphoreType.DMA((count,))],
    )(pos, mask, x, *pieces)


def down_gradient(pos, mask, pieces, x):
    tokens, width = x.shape
    units = pieces[0].shape[1]
    size = tokens // 4
    count = units // CHUNK

    def kernel(pos_ref, mask_ref, *refs):
        parts, (x_ref, out, lhs, rhs, result, sems) = refs[: len(pieces)], refs[len(pieces) :]
        for k in range(4):
            rhs[k * size : (k + 1) * size] = token_rows(pos_ref, x_ref, k)
        gather_rows(parts, lhs)
        copies = []
        for i in range(count):
            full = lax.dot_general(
                lhs[:, i * CHUNK : (i + 1) * CHUNK], rhs[...], dims(0, 0), preferred_element_type=F32
            )
            chunk_of(result, i, True)[...] = masked(full, mask_ref, i * (CHUNK // BLOCK), 0).astype(BF16)
            copies.append(pltpu.make_async_copy(chunk_of(result, i, True), chunk_of(out, i, True), sems.at[i]))
            copies[-1].start()
        for copy in copies:
            copy.wait()

    return call(
        kernel, [SMEM, SMEM] + [VMEM] * len(pieces) + [VMEM], HBM,
        jax.ShapeDtypeStruct((units, width), BF16),
        [pltpu.VMEM((tokens, units), BF16), pltpu.VMEM((tokens, width), BF16), pltpu.VMEM((units, width), BF16),
         pltpu.SemaphoreType.DMA((count,))],
    )(pos, mask, *pieces, x)


def y_joined(pos, pieces):
    size, width = pieces[0].shape

    def kernel(pos_ref, *refs):
        for k in range(4):
            at = pl.multiple_of((pos_ref[1] + k) % 4 * size, size)
            refs[4][pl.ds(at, size), :] = refs[k][...]

    return call(kernel, [SMEM] + [VMEM] * 4, VMEM, jax.ShapeDtypeStruct((4 * size, width), BF16))(pos, *pieces)


def all_rows(pos, mine, other):
    half, width = mine.shape
    size = half // 2

    def kernel(pos_ref, mine_ref, other_ref, out, sems):
        z, core = pos_ref[0], pos_ref[2]
        copies = []
        for side, ref in enumerate((mine_ref, other_ref)):
            for k in range(2):
                first = 2 * core if side == 0 else 2 - 2 * core
                to = pl.multiple_of((z + first + k) % 4 * size, size)
                copies.append(
                    pltpu.make_async_copy(ref.at[pl.ds(k * size, size), :], out.at[pl.ds(to, size), :], sems.at[2 * side + k])
                )
        for copy in copies:
            copy.start()
        for copy in copies:
            copy.wait()

    return call(
        kernel, [SMEM, VMEM, VMEM], HBM, jax.ShapeDtypeStruct((2 * half, width), BF16),
        [pltpu.SemaphoreType.DMA((4,))],
    )(pos, mine, other)


def col_reduce(pos, kept, sent):
    mine = kept + col_send(sent, CORE_SWAP).astype(F32)
    own, nxt, far, prv = jnp.split(mine, 4, axis=0)
    a = col_send(far.astype(BF16), y_step(2))
    b = col_send(nxt.astype(BF16), y_step(1))
    c = col_send(prv.astype(BF16), y_step(-1))
    own = (own + a.astype(F32) + b.astype(F32) + c.astype(F32)).astype(BF16)
    own = (own.astype(F32) + col_send(own, H_SWAP).astype(F32)).astype(BF16)
    far = col_send(own, y_step(2))
    prv = col_send(own, y_step(1))
    nxt = col_send(own, y_step(-1))
    mine = y_joined(pos, (own, nxt, far, prv))
    return all_rows(pos, mine, col_send(mine, CORE_SWAP))


def activate(value):
    return jax.nn.gelu(value, approximate=True)


def activated(part, arrived):
    def kernel(part_ref, arrived_ref, active, slope):
        value, pull_back = jax.vjp(activate, part_ref[...] + arrived_ref[...].astype(F32))
        active[...] = value.astype(BF16)
        slope[...] = pull_back(jnp.ones_like(value))[0]

    return call(
        kernel, [VMEM] * 2, [VMEM] * 2,
        [jax.ShapeDtypeStruct(part.shape, BF16), jax.ShapeDtypeStruct(part.shape, F32)],
    )(part, arrived)


def body(inputs, up_weight, down_weight, up_mask, down_mask, cotangent):
    col = lax.axis_index("col")
    pos = jnp.stack([lax.axis_index("row") % 4, col // 2 % 4, col % 2]).astype(jnp.int32)
    far_a, far_b, masked_up = hidden_far(pos, up_mask, inputs, up_weight)
    hidden = z_reduce((far_a, far_b, *hidden_near(pos, inputs, masked_up)))
    active_own, slope = activated(hidden, x_swap(hidden))
    active = z_collect(active_own)
    *grad_pieces, masked_down = grad_part(pos, down_mask, cotangent, down_weight)
    grad = z_reduce(grad_pieces)
    hidden_grad = z_collect(((grad + x_swap(grad).astype(F32)) * slope).astype(BF16))
    output = col_reduce(pos, *down_part(pos, active, masked_down, False))
    input_grad = col_reduce(pos, *down_part(pos, hidden_grad, masked_up, True))
    down_grad = down_gradient(pos, down_mask, active, cotangent)
    up_grad = up_gradient(pos, up_mask, inputs, hidden_grad)
    return (output, input_grad, up_grad, down_grad)


def solution(mesh):
    in_specs = (
        P(None, "row"),
        P("row", "col"),
        P("col", "row"),
        P("row", "col"),
        P("col", "row"),
        P(None, "row"),
    )
    out_specs = (P(None, "row"), P(None, "row"), P("row", "col"), P("col", "row"))
    return jax.shard_map(body, mesh=mesh, in_specs=in_specs, out_specs=out_specs, check_vma=False)
```

```python
import jax
import jax.numpy as jnp
from jax import lax
from jax.experimental import pallas as pl
from jax.experimental.pallas import tpu as pltpu
from jax.sharding import PartitionSpec as P


F32 = jnp.float32
BF16 = jnp.bfloat16
BLOCK = 128


def z_step(d):
    return [(x * 4 + z, x * 4 + (z + d) % 4) for x in range(2) for z in range(4)]


def y_step(d):
    return [(h * 8 + y * 2 + c, h * 8 + (y + d) % 4 * 2 + c) for h in range(2) for y in range(4) for c in range(2)]


X_SWAP = [(i, i ^ 4) for i in range(8)]
CORE_SWAP = [(i, i ^ 1) for i in range(16)]
H_SWAP = [(i, i ^ 8) for i in range(16)]


def row_send(v, perm):
    return lax.ppermute(v, "row", perm)


def col_send(v, perm):
    return lax.ppermute(v, "col", perm)


def masked(w, mask_ref, row0, col0):
    rows = []
    for r in range(w.shape[0] // BLOCK):
        row = w[r * BLOCK : (r + 1) * BLOCK]
        cols = []
        for c in range(w.shape[1] // BLOCK):
            piece = row[:, c * BLOCK : (c + 1) * BLOCK]
            cols.append(jnp.where(mask_ref[row0 + r, col0 + c] > 0, piece, jnp.zeros_like(piece)))
        rows.append(jnp.concatenate(cols, axis=1))
    return jnp.concatenate(rows, axis=0)


def dims(lhs, rhs):
    return (((lhs,), (rhs,)), ((), ()))


VMEM = pl.BlockSpec(memory_space=pltpu.VMEM)
SMEM = pl.BlockSpec(memory_space=pltpu.SMEM)
HBM = pl.BlockSpec(memory_space=pltpu.HBM)
CHUNK = 256
FETCH_LIMIT = 48


def call(body, in_specs, out_specs, out_shape, scratch=(), limit=20):
    return pl.pallas_call(
        body,
        in_specs=in_specs,
        out_specs=out_specs,
        out_shape=out_shape,
        scratch_shapes=scratch,
        compiler_params=pltpu.CompilerParams(vmem_limit_bytes=limit * 1024 * 1024),
    )


def chunk_of(ref, i, rows):
    at = pl.ds(i * CHUNK, CHUNK)
    return ref.at[at, :] if rows else ref.at[:, at]


def spans(size, widths):
    at = 0
    for width in widths:
        width = min(width, size - at)
        if width:
            yield at, width
        at += width
    if at < size:
        yield at, size - at


def span_of(ref, span, rows):
    return ref.at[pl.ds(*span), :] if rows else ref.at[:, pl.ds(*span)]


def times_span(lhs, w, mask_ref, span, rows, kept=None):
    first = span[0] // BLOCK
    tile = masked(span_of(w, span, rows)[...], mask_ref, *((first, 0) if rows else (0, first)))
    if kept is not None:
        span_of(kept, span, rows)[...] = tile
    return lax.dot_general(lhs, tile, dims(1, 1 if rows else 0), preferred_element_type=F32)


def row_fetches(z, x_hbm, x_ref, sems, blocks):
    tokens = x_hbm.shape[0] // 4
    copies = []
    for i, k in enumerate(blocks):
        at = pl.multiple_of((z + k) % 4 * tokens, tokens)
        to = pl.ds(i * tokens, tokens)
        copies.append(pltpu.make_async_copy(x_hbm.at[pl.ds(at, tokens), :], x_ref.at[to, :], sems.at[i]))
    return copies


def hidden_far(pos, mask, x, w):
    units = w.shape[1]
    tokens = x.shape[0] // 4
    half = tokens // 2
    parts = list(spans(units, (256, 512, 512)))

    def kernel(pos_ref, mask_ref, x_hbm, w_hbm, far_a, far_b, kept, x_ref, w_ref, x_sems, sems):
        x_copies = row_fetches(pos_ref[0], x_hbm, x_ref, x_sems, (2,))
        copies = [
            pltpu.make_async_copy(span_of(w_hbm, s, False), span_of(w_ref, s, False), sems.at[i])
            for i, s in enumerate(parts)
        ]
        for copy in x_copies + copies:
            copy.start()
        x_copies[0].wait()
        for copy, span in zip(copies, parts):
            copy.wait()
            far = times_span(x_ref[...], w_ref, mask_ref, span, False, kept).astype(BF16)
            far_a[:, pl.ds(*span)] = far[:half]
            far_b[:, pl.ds(*span)] = far[half:]

    return call(
        kernel, [SMEM, SMEM, HBM, HBM], [VMEM] * 3,
        [jax.ShapeDtypeStruct((half, units), BF16)] * 2 + [jax.ShapeDtypeStruct(w.shape, BF16)],
        [pltpu.VMEM((tokens, x.shape[1]), BF16), pltpu.VMEM(w.shape, BF16), pltpu.SemaphoreType.DMA((1,)),
         pltpu.SemaphoreType.DMA((len(parts),))],
        limit=FETCH_LIMIT,
    )(pos, mask, x, w)


def hidden_near(pos, x, w):
    units = w.shape[1]
    tokens = x.shape[0] // 4

    def kernel(pos_ref, x_hbm, w_ref, own, nxt, prv, x_ref, x_sems):
        x_copies = row_fetches(pos_ref[0], x_hbm, x_ref, x_sems, (0, 1, 3))
        for copy in x_copies:
            copy.start()
        for copy in x_copies:
            copy.wait()
        for span in spans(units, (896, 896)):
            at = pl.ds(*span)
            part = lax.dot_general(x_ref[...], w_ref[:, at], dims(1, 0), preferred_element_type=F32)
            own[:, at] = part[:tokens]
            nxt[:, at] = part[tokens : 2 * tokens]
            prv[:, at] = part[2 * tokens :]

    return call(
        kernel, [SMEM, HBM, VMEM], [VMEM] * 3, [jax.ShapeDtypeStruct((tokens, units), F32)] * 3,
        [pltpu.VMEM((3 * tokens, x.shape[1]), BF16), pltpu.SemaphoreType.DMA((3,))],
    )(pos, x, w)


def grad_part(pos, mask, x, w):
    units = w.shape[0]
    tokens = x.shape[0] // 4
    half = tokens // 2
    parts = list(spans(units, (512, 512, 768)))

    def kernel(pos_ref, mask_ref, x_hbm, w_hbm, far_a, far_b, own, nxt, prv, x_ref, w_ref, x_sems, sems):
        x_copies = row_fetches(pos_ref[0], x_hbm, x_ref, x_sems, (0, 1, 2, 3))
        copies = [
            pltpu.make_async_copy(span_of(w_hbm, s, True), span_of(w_ref, s, True), sems.at[i])
            for i, s in enumerate(parts)
        ]
        for copy in x_copies + copies:
            copy.start()
        for copy in x_copies:
            copy.wait()
        for copy, span in zip(copies, parts):
            copy.wait()
            at = pl.ds(*span)
            part = times_span(x_ref[...], w_ref, mask_ref, span, True)
            own[:, at] = part[:tokens]
            nxt[:, at] = part[tokens : 2 * tokens]
            far = part[2 * tokens : 3 * tokens].astype(BF16)
            far_a[:, at] = far[:half]
            far_b[:, at] = far[half:]
            prv[:, at] = part[3 * tokens :]

    return call(
        kernel, [SMEM, SMEM, HBM, HBM], [VMEM] * 5,
        [jax.ShapeDtypeStruct((half, units), BF16)] * 2 + [jax.ShapeDtypeStruct((tokens, units), F32)] * 3,
        [pltpu.VMEM(x.shape, BF16), pltpu.VMEM(w.shape, BF16), pltpu.SemaphoreType.DMA((4,)),
         pltpu.SemaphoreType.DMA((len(parts),))],
        limit=FETCH_LIMIT,
    )(pos, mask, x, w)


def joined(nxt, prv, from_prv, from_nxt):
    tokens, units = nxt.shape
    half = tokens // 2

    def kernel(nxt_ref, prv_ref, a_ref, b_ref, up, down):
        up[:half] = (nxt_ref[:half] + a_ref[...].astype(F32)).astype(BF16)
        up[half:] = nxt_ref[half:].astype(BF16)
        down[:half] = prv_ref[:half].astype(BF16)
        down[half:] = (prv_ref[half:] + b_ref[...].astype(F32)).astype(BF16)

    return call(
        kernel, [VMEM] * 4, [VMEM] * 2, [jax.ShapeDtypeStruct((tokens, units), BF16)] * 2
    )(nxt, prv, from_prv, from_nxt)


def z_reduce(pieces):
    far_a, far_b, own, nxt, prv = pieces
    from_prv = row_send(far_a, z_step(1))
    from_nxt = row_send(far_b, z_step(-1))
    up, down = joined(nxt, prv, from_prv, from_nxt)
    a = row_send(up, z_step(1))
    b = row_send(down, z_step(-1))
    return own + a.astype(F32) + b.astype(F32)


def x_swap(part):
    return row_send(part.astype(BF16), X_SWAP)


def z_collect(own):
    half = own.shape[0] // 2
    prv = row_send(own, z_step(1))
    nxt = row_send(own, z_step(-1))
    far_a = row_send(nxt[:half], z_step(-1))
    far_b = row_send(prv[half:], z_step(1))
    return own, nxt, far_a, far_b, prv


def gather_rows(refs, scratch):
    at = 0
    for ref in refs:
        scratch[at : at + ref.shape[0]] = ref[...]
        at += ref.shape[0]


def down_part(pos, mask, pieces, w, transposed):
    width = w.shape[0] if transposed else w.shape[1]
    units = w.shape[1] if transposed else w.shape[0]
    tokens = sum(p.shape[0] for p in pieces)
    half, size = tokens // 2, tokens // 8

    def kernel(pos_ref, mask_ref, *refs):
        parts, (w_ref, kept, sent, lhs) = refs[: len(pieces)], refs[len(pieces) :]
        y, core = pos_ref[1], pos_ref[2]
        block = 0
        for part in parts:
            for at in range(0, part.shape[0], size):
                side = core if block < 4 else 1 - core
                to = pl.multiple_of(side * half + (block + 4 - y) % 4 * size, size)
                lhs[pl.ds(to, size), :] = part[at : at + size, :]
                block += 1
        for span in spans(width, (512, 512)):
            full = times_span(lhs[...], w_ref, mask_ref, span, transposed)
            kept[:, pl.ds(*span)] = full[:half]
            sent[:, pl.ds(*span)] = full[half:].astype(BF16)

    return call(
        kernel, [SMEM, SMEM] + [VMEM] * (len(pieces) + 1), [VMEM] * 2,
        [jax.ShapeDtypeStruct((half, width), F32), jax.ShapeDtypeStruct((half, width), BF16)],
        [pltpu.VMEM((tokens, units), BF16)],
    )(pos, mask, *pieces, w)


def token_rows(pos_ref, x_ref, k):
    size = x_ref.shape[0] // 4
    return x_ref[pl.ds(pl.multiple_of((pos_ref[0] + k) % 4 * size, size), size), :]


def up_gradient(pos, mask, x, pieces):
    tokens, width = x.shape
    units = pieces[0].shape[1]
    size = tokens // 4
    count = units // CHUNK

    def kernel(pos_ref, mask_ref, x_ref, *refs):
        parts, (out, lhs, rhs, result, sems) = refs[: len(pieces)], refs[len(pieces) :]
        for k in range(4):
            lhs[:, k * size : (k + 1) * size] = token_rows(pos_ref, x_ref, k).T
        gather_rows(parts, rhs)
        copies = []
        for i in range(count):
            full = lax.dot_general(
                lhs[...], rhs[:, i * CHUNK : (i + 1) * CHUNK], dims(1, 0), preferred_element_type=F32
            )
            chunk_of(result, i, False)[...] = masked(full, mask_ref, 0, i * (CHUNK // BLOCK)).astype(BF16)
            copies.append(pltpu.make_async_copy(chunk_of(result, i, False), chunk_of(out, i, False), sems.at[i]))
            copies[-1].start()
        for copy in copies:
            copy.wait()

    return call(
        kernel, [SMEM, SMEM, VMEM] + [VMEM] * len(pieces), HBM, jax.ShapeDtypeStruct((width, units), BF16),
        [pltpu.VMEM((width, tokens), BF16), pltpu.VMEM((tokens, units), BF16), pltpu.VMEM((width, units), BF16),
         pltpu.SemaphoreType.DMA((count,))],
    )(pos, mask, x, *pieces)


def down_gradient(pos, mask, pieces, x):
    tokens, width = x.shape
    units = pieces[0].shape[1]
    size = tokens // 4
    count = units // CHUNK

    def kernel(pos_ref, mask_ref, *refs):
        parts, (x_ref, out, lhs, rhs, result, sems) = refs[: len(pieces)], refs[len(pieces) :]
        for k in range(4):
            rhs[k * size : (k + 1) * size] = token_rows(pos_ref, x_ref, k)
        gather_rows(parts, lhs)
        copies = []
        for i in range(count):
            full = lax.dot_general(
                lhs[:, i * CHUNK : (i + 1) * CHUNK], rhs[...], dims(0, 0), preferred_element_type=F32
            )
            chunk_of(result, i, True)[...] = masked(full, mask_ref, i * (CHUNK // BLOCK), 0).astype(BF16)
            copies.append(pltpu.make_async_copy(chunk_of(result, i, True), chunk_of(out, i, True), sems.at[i]))
            copies[-1].start()
        for copy in copies:
            copy.wait()

    return call(
        kernel, [SMEM, SMEM] + [VMEM] * len(pieces) + [VMEM], HBM,
        jax.ShapeDtypeStruct((units, width), BF16),
        [pltpu.VMEM((tokens, units), BF16), pltpu.VMEM((tokens, width), BF16), pltpu.VMEM((units, width), BF16),
         pltpu.SemaphoreType.DMA((count,))],
    )(pos, mask, *pieces, x)


def y_joined(pos, pieces):
    size, width = pieces[0].shape

    def kernel(pos_ref, *refs):
        for k in range(4):
            at = pl.multiple_of((pos_ref[1] + k) % 4 * size, size)
            refs[4][pl.ds(at, size), :] = refs[k][...]

    return call(kernel, [SMEM] + [VMEM] * 4, VMEM, jax.ShapeDtypeStruct((4 * size, width), BF16))(pos, *pieces)


def all_rows(pos, mine, other):
    half, width = mine.shape
    size = half // 2

    def kernel(pos_ref, mine_ref, other_ref, out, sems):
        z, core = pos_ref[0], pos_ref[2]
        copies = []
        for side, ref in enumerate((mine_ref, other_ref)):
            for k in range(2):
                first = 2 * core if side == 0 else 2 - 2 * core
                to = pl.multiple_of((z + first + k) % 4 * size, size)
                copies.append(
                    pltpu.make_async_copy(ref.at[pl.ds(k * size, size), :], out.at[pl.ds(to, size), :], sems.at[2 * side + k])
                )
        for copy in copies:
            copy.start()
        for copy in copies:
            copy.wait()

    return call(
        kernel, [SMEM, VMEM, VMEM], HBM, jax.ShapeDtypeStruct((2 * half, width), BF16),
        [pltpu.SemaphoreType.DMA((4,))],
    )(pos, mine, other)


def col_reduce(pos, kept, sent):
    mine = kept + col_send(sent, CORE_SWAP).astype(F32)
    own, nxt, far, prv = jnp.split(mine, 4, axis=0)
    a = col_send(far.astype(BF16), y_step(2))
    b = col_send(nxt.astype(BF16), y_step(1))
    c = col_send(prv.astype(BF16), y_step(-1))
    own = (own + a.astype(F32) + b.astype(F32) + c.astype(F32)).astype(BF16)
    own = (own.astype(F32) + col_send(own, H_SWAP).astype(F32)).astype(BF16)
    far = col_send(own, y_step(2))
    prv = col_send(own, y_step(1))
    nxt = col_send(own, y_step(-1))
    mine = y_joined(pos, (own, nxt, far, prv))
    return all_rows(pos, mine, col_send(mine, CORE_SWAP))


def activate(value):
    return jax.nn.gelu(value, approximate=True)


def activated(part, arrived):
    def kernel(part_ref, arrived_ref, active, slope):
        value, pull_back = jax.vjp(activate, part_ref[...] + arrived_ref[...].astype(F32))
        active[...] = value.astype(BF16)
        slope[...] = pull_back(jnp.ones_like(value))[0]

    return call(
        kernel, [VMEM] * 2, [VMEM] * 2,
        [jax.ShapeDtypeStruct(part.shape, BF16), jax.ShapeDtypeStruct(part.shape, F32)],
    )(part, arrived)


def body(inputs, up_weight, down_weight, up_mask, down_mask, cotangent):
    col = lax.axis_index("col")
    pos = jnp.stack([lax.axis_index("row") % 4, col // 2 % 4, col % 2]).astype(jnp.int32)
    far_a, far_b, masked_up = hidden_far(pos, up_mask, inputs, up_weight)
    hidden = z_reduce((far_a, far_b, *hidden_near(pos, inputs, masked_up)))
    active_own, slope = activated(hidden, x_swap(hidden))
    active = z_collect(active_own)
    grad = z_reduce(grad_part(pos, down_mask, cotangent, down_weight))
    hidden_grad = z_collect(((grad + x_swap(grad).astype(F32)) * slope).astype(BF16))
    output = col_reduce(pos, *down_part(pos, down_mask, active, down_weight, False))
    input_grad = col_reduce(pos, *down_part(pos, up_mask, hidden_grad, up_weight, True))
    down_grad = down_gradient(pos, down_mask, active, cotangent)
    up_grad = up_gradient(pos, up_mask, inputs, hidden_grad)
    return (output, input_grad, up_grad, down_grad)


def solution(mesh):
    in_specs = (
        P(None, "row"),
        P("row", "col"),
        P("col", "row"),
        P("row", "col"),
        P("col", "row"),
        P(None, "row"),
    )
    out_specs = (P(None, "row"), P(None, "row"), P("row", "col"), P("col", "row"))
    return jax.shard_map(body, mesh=mesh, in_specs=in_specs, out_specs=out_specs, check_vma=False)
```

```python
import jax
import jax.numpy as jnp
from jax import lax
from jax.experimental import pallas as pl
from jax.experimental.pallas import tpu as pltpu
from jax.sharding import PartitionSpec as P


F32 = jnp.float32
BF16 = jnp.bfloat16
BLOCK = 128


def z_step(d):
    return [(x * 4 + z, x * 4 + (z + d) % 4) for x in range(2) for z in range(4)]


def y_step(d):
    return [(h * 8 + y * 2 + c, h * 8 + (y + d) % 4 * 2 + c) for h in range(2) for y in range(4) for c in range(2)]


X_SWAP = [(i, i ^ 4) for i in range(8)]
CORE_SWAP = [(i, i ^ 1) for i in range(16)]
H_SWAP = [(i, i ^ 8) for i in range(16)]


def row_send(v, perm):
    return lax.ppermute(v, "row", perm)


def col_send(v, perm):
    return lax.ppermute(v, "col", perm)


def masked(w, mask_ref, row0, col0):
    rows = []
    for r in range(w.shape[0] // BLOCK):
        row = w[r * BLOCK : (r + 1) * BLOCK]
        cols = []
        for c in range(w.shape[1] // BLOCK):
            piece = row[:, c * BLOCK : (c + 1) * BLOCK]
            cols.append(jnp.where(mask_ref[row0 + r, col0 + c] > 0, piece, jnp.zeros_like(piece)))
        rows.append(jnp.concatenate(cols, axis=1))
    return jnp.concatenate(rows, axis=0)


def dims(lhs, rhs):
    return (((lhs,), (rhs,)), ((), ()))


VMEM = pl.BlockSpec(memory_space=pltpu.VMEM)
SMEM = pl.BlockSpec(memory_space=pltpu.SMEM)
HBM = pl.BlockSpec(memory_space=pltpu.HBM)
CHUNK = 256
FETCH_LIMIT = 48
FIRST_LIMIT = 48


def call(body, in_specs, out_specs, out_shape, scratch=(), limit=20):
    return pl.pallas_call(
        body,
        in_specs=in_specs,
        out_specs=out_specs,
        out_shape=out_shape,
        scratch_shapes=scratch,
        compiler_params=pltpu.CompilerParams(vmem_limit_bytes=limit * 1024 * 1024),
    )


def chunk_of(ref, i, rows):
    at = pl.ds(i * CHUNK, CHUNK)
    return ref.at[at, :] if rows else ref.at[:, at]


def spans(size, widths):
    at = 0
    for width in widths:
        width = min(width, size - at)
        if width:
            yield at, width
        at += width
    if at < size:
        yield at, size - at


def span_of(ref, span, rows):
    return ref.at[pl.ds(*span), :] if rows else ref.at[:, pl.ds(*span)]


def times_span(lhs, w, mask_ref, span, rows, kept=None):
    first = span[0] // BLOCK
    tile = masked(span_of(w, span, rows)[...], mask_ref, *((first, 0) if rows else (0, first)))
    if kept is not None:
        span_of(kept, span, rows)[...] = tile
    return lax.dot_general(lhs, tile, dims(1, 1 if rows else 0), preferred_element_type=F32)


def row_fetches(z, x_hbm, x_ref, sems, blocks):
    tokens = x_hbm.shape[0] // 4
    copies = []
    for i, k in enumerate(blocks):
        at = pl.multiple_of((z + k) % 4 * tokens, tokens)
        to = pl.ds(i * tokens, tokens)
        copies.append(pltpu.make_async_copy(x_hbm.at[pl.ds(at, tokens), :], x_ref.at[to, :], sems.at[i]))
    return copies


def hidden_far(pos, mask, x, w):
    units = w.shape[1]
    tokens = x.shape[0] // 4
    half = tokens // 2
    parts = list(spans(units, (256, 512, 512)))

    def kernel(pos_ref, mask_ref, x_hbm, w_hbm, far_a, far_b, kept, x_ref, w_ref, x_sems, sems):
        x_copies = row_fetches(pos_ref[0], x_hbm, x_ref, x_sems, (2,))
        copies = [
            pltpu.make_async_copy(span_of(w_hbm, s, False), span_of(w_ref, s, False), sems.at[i])
            for i, s in enumerate(parts)
        ]
        for copy in x_copies + copies:
            copy.start()
        x_copies[0].wait()
        for copy, span in zip(copies, parts):
            copy.wait()
            far = times_span(x_ref[...], w_ref, mask_ref, span, False, kept).astype(BF16)
            far_a[:, pl.ds(*span)] = far[:half]
            far_b[:, pl.ds(*span)] = far[half:]

    return call(
        kernel, [SMEM, SMEM, HBM, HBM], [VMEM] * 3,
        [jax.ShapeDtypeStruct((half, units), BF16)] * 2 + [jax.ShapeDtypeStruct(w.shape, BF16)],
        [pltpu.VMEM((tokens, x.shape[1]), BF16), pltpu.VMEM(w.shape, BF16), pltpu.SemaphoreType.DMA((1,)),
         pltpu.SemaphoreType.DMA((len(parts),))],
        limit=FIRST_LIMIT,
    )(pos, mask, x, w)


def hidden_near(pos, x, w):
    units = w.shape[1]
    tokens = x.shape[0] // 4

    def kernel(pos_ref, x_hbm, w_ref, own, nxt, prv, x_ref, x_sems):
        x_copies = row_fetches(pos_ref[0], x_hbm, x_ref, x_sems, (0, 1, 3))
        for copy in x_copies:
            copy.start()
        for copy in x_copies:
            copy.wait()
        for span in spans(units, (896, 896)):
            at = pl.ds(*span)
            part = lax.dot_general(x_ref[...], w_ref[:, at], dims(1, 0), preferred_element_type=F32)
            own[:, at] = part[:tokens]
            nxt[:, at] = part[tokens : 2 * tokens]
            prv[:, at] = part[2 * tokens :]

    return call(
        kernel, [SMEM, HBM, VMEM], [VMEM] * 3, [jax.ShapeDtypeStruct((tokens, units), F32)] * 3,
        [pltpu.VMEM((3 * tokens, x.shape[1]), BF16), pltpu.SemaphoreType.DMA((3,))],
    )(pos, x, w)


def grad_part(pos, mask, x, w):
    units = w.shape[0]
    tokens = x.shape[0] // 4
    half = tokens // 2
    parts = list(spans(units, (512, 512, 768)))

    def kernel(pos_ref, mask_ref, x_hbm, w_hbm, far_a, far_b, own, nxt, prv, x_ref, w_ref, x_sems, sems):
        x_copies = row_fetches(pos_ref[0], x_hbm, x_ref, x_sems, (0, 1, 2, 3))
        copies = [
            pltpu.make_async_copy(span_of(w_hbm, s, True), span_of(w_ref, s, True), sems.at[i])
            for i, s in enumerate(parts)
        ]
        for copy in x_copies + copies:
            copy.start()
        for copy in x_copies:
            copy.wait()
        for copy, span in zip(copies, parts):
            copy.wait()
            at = pl.ds(*span)
            part = times_span(x_ref[...], w_ref, mask_ref, span, True)
            own[:, at] = part[:tokens]
            nxt[:, at] = part[tokens : 2 * tokens]
            far = part[2 * tokens : 3 * tokens].astype(BF16)
            far_a[:, at] = far[:half]
            far_b[:, at] = far[half:]
            prv[:, at] = part[3 * tokens :]

    return call(
        kernel, [SMEM, SMEM, HBM, HBM], [VMEM] * 5,
        [jax.ShapeDtypeStruct((half, units), BF16)] * 2 + [jax.ShapeDtypeStruct((tokens, units), F32)] * 3,
        [pltpu.VMEM(x.shape, BF16), pltpu.VMEM(w.shape, BF16), pltpu.SemaphoreType.DMA((4,)),
         pltpu.SemaphoreType.DMA((len(parts),))],
        limit=FETCH_LIMIT,
    )(pos, mask, x, w)


def joined(nxt, prv, from_prv, from_nxt):
    tokens, units = nxt.shape
    half = tokens // 2

    def kernel(nxt_ref, prv_ref, a_ref, b_ref, up, down):
        up[:half] = (nxt_ref[:half] + a_ref[...].astype(F32)).astype(BF16)
        up[half:] = nxt_ref[half:].astype(BF16)
        down[:half] = prv_ref[:half].astype(BF16)
        down[half:] = (prv_ref[half:] + b_ref[...].astype(F32)).astype(BF16)

    return call(
        kernel, [VMEM] * 4, [VMEM] * 2, [jax.ShapeDtypeStruct((tokens, units), BF16)] * 2
    )(nxt, prv, from_prv, from_nxt)


def z_reduce(pieces):
    far_a, far_b, own, nxt, prv = pieces
    from_prv = row_send(far_a, z_step(1))
    from_nxt = row_send(far_b, z_step(-1))
    up, down = joined(nxt, prv, from_prv, from_nxt)
    a = row_send(up, z_step(1))
    b = row_send(down, z_step(-1))
    return own + a.astype(F32) + b.astype(F32)


def x_swap(part):
    return row_send(part.astype(BF16), X_SWAP)


def z_collect(own):
    half = own.shape[0] // 2
    prv = row_send(own, z_step(1))
    nxt = row_send(own, z_step(-1))
    far_a = row_send(nxt[:half], z_step(-1))
    far_b = row_send(prv[half:], z_step(1))
    return own, nxt, far_a, far_b, prv


def gather_rows(refs, scratch):
    at = 0
    for ref in refs:
        scratch[at : at + ref.shape[0]] = ref[...]
        at += ref.shape[0]


def down_part(pos, mask, pieces, w, transposed):
    width = w.shape[0] if transposed else w.shape[1]
    units = w.shape[1] if transposed else w.shape[0]
    tokens = sum(p.shape[0] for p in pieces)
    half, size = tokens // 2, tokens // 8

    def kernel(pos_ref, mask_ref, *refs):
        parts, (w_ref, kept, sent, lhs) = refs[: len(pieces)], refs[len(pieces) :]
        y, core = pos_ref[1], pos_ref[2]
        block = 0
        for part in parts:
            for at in range(0, part.shape[0], size):
                side = core if block < 4 else 1 - core
                to = pl.multiple_of(side * half + (block + 4 - y) % 4 * size, size)
                lhs[pl.ds(to, size), :] = part[at : at + size, :]
                block += 1
        for span in spans(width, (512, 512)):
            full = times_span(lhs[...], w_ref, mask_ref, span, transposed)
            kept[:, pl.ds(*span)] = full[:half]
            sent[:, pl.ds(*span)] = full[half:].astype(BF16)

    return call(
        kernel, [SMEM, SMEM] + [VMEM] * (len(pieces) + 1), [VMEM] * 2,
        [jax.ShapeDtypeStruct((half, width), F32), jax.ShapeDtypeStruct((half, width), BF16)],
        [pltpu.VMEM((tokens, units), BF16)],
    )(pos, mask, *pieces, w)


def token_rows(pos_ref, x_ref, k):
    size = x_ref.shape[0] // 4
    return x_ref[pl.ds(pl.multiple_of((pos_ref[0] + k) % 4 * size, size), size), :]


def up_gradient(pos, mask, x, pieces):
    tokens, width = x.shape
    units = pieces[0].shape[1]
    size = tokens // 4
    count = units // CHUNK

    def kernel(pos_ref, mask_ref, x_ref, *refs):
        parts, (out, lhs, rhs, result, sems) = refs[: len(pieces)], refs[len(pieces) :]
        for k in range(4):
            lhs[:, k * size : (k + 1) * size] = token_rows(pos_ref, x_ref, k).T
        gather_rows(parts, rhs)
        copies = []
        for i in range(count):
            full = lax.dot_general(
                lhs[...], rhs[:, i * CHUNK : (i + 1) * CHUNK], dims(1, 0), preferred_element_type=F32
            )
            chunk_of(result, i, False)[...] = masked(full, mask_ref, 0, i * (CHUNK // BLOCK)).astype(BF16)
            copies.append(pltpu.make_async_copy(chunk_of(result, i, False), chunk_of(out, i, False), sems.at[i]))
            copies[-1].start()
        for copy in copies:
            copy.wait()

    return call(
        kernel, [SMEM, SMEM, VMEM] + [VMEM] * len(pieces), HBM, jax.ShapeDtypeStruct((width, units), BF16),
        [pltpu.VMEM((width, tokens), BF16), pltpu.VMEM((tokens, units), BF16), pltpu.VMEM((width, units), BF16),
         pltpu.SemaphoreType.DMA((count,))],
    )(pos, mask, x, *pieces)


def down_gradient(pos, mask, pieces, x):
    tokens, width = x.shape
    units = pieces[0].shape[1]
    size = tokens // 4
    count = units // CHUNK

    def kernel(pos_ref, mask_ref, *refs):
        parts, (x_ref, out, lhs, rhs, result, sems) = refs[: len(pieces)], refs[len(pieces) :]
        for k in range(4):
            rhs[k * size : (k + 1) * size] = token_rows(pos_ref, x_ref, k)
        gather_rows(parts, lhs)
        copies = []
        for i in range(count):
            full = lax.dot_general(
                lhs[:, i * CHUNK : (i + 1) * CHUNK], rhs[...], dims(0, 0), preferred_element_type=F32
            )
            chunk_of(result, i, True)[...] = masked(full, mask_ref, i * (CHUNK // BLOCK), 0).astype(BF16)
            copies.append(pltpu.make_async_copy(chunk_of(result, i, True), chunk_of(out, i, True), sems.at[i]))
            copies[-1].start()
        for copy in copies:
            copy.wait()

    return call(
        kernel, [SMEM, SMEM] + [VMEM] * len(pieces) + [VMEM], HBM,
        jax.ShapeDtypeStruct((units, width), BF16),
        [pltpu.VMEM((tokens, units), BF16), pltpu.VMEM((tokens, width), BF16), pltpu.VMEM((units, width), BF16),
         pltpu.SemaphoreType.DMA((count,))],
    )(pos, mask, *pieces, x)


def y_joined(pos, pieces):
    size, width = pieces[0].shape

    def kernel(pos_ref, *refs):
        for k in range(4):
            at = pl.multiple_of((pos_ref[1] + k) % 4 * size, size)
            refs[4][pl.ds(at, size), :] = refs[k][...]

    return call(kernel, [SMEM] + [VMEM] * 4, VMEM, jax.ShapeDtypeStruct((4 * size, width), BF16))(pos, *pieces)


def all_rows(pos, *halves):
    half, width = halves[0].shape
    size = half // 2
    results = len(halves) // 2

    def kernel(pos_ref, *refs):
        sources, outs, sems = refs[: 2 * results], refs[2 * results : -1], refs[-1]
        z, core = pos_ref[0], pos_ref[2]
        copies = []
        for i, ref in enumerate(sources):
            for k in range(2):
                first = 2 * core if i % 2 == 0 else 2 - 2 * core
                to = pl.multiple_of((z + first + k) % 4 * size, size)
                rows = pl.ds(k * size, size)
                copies.append(
                    pltpu.make_async_copy(ref.at[rows, :], outs[i // 2].at[pl.ds(to, size), :], sems.at[2 * i + k])
                )
        for copy in copies:
            copy.start()
        for copy in copies:
            copy.wait()

    return call(
        kernel, [SMEM] + [VMEM] * (2 * results), [HBM] * results,
        [jax.ShapeDtypeStruct((2 * half, width), BF16)] * results, [pltpu.SemaphoreType.DMA((4 * results,))],
    )(pos, *halves)


def col_reduce(pos, kept, sent):
    mine = kept + col_send(sent, CORE_SWAP).astype(F32)
    own, nxt, far, prv = jnp.split(mine, 4, axis=0)
    a = col_send(far.astype(BF16), y_step(2))
    b = col_send(nxt.astype(BF16), y_step(1))
    c = col_send(prv.astype(BF16), y_step(-1))
    own = (own + a.astype(F32) + b.astype(F32) + c.astype(F32)).astype(BF16)
    own = (own.astype(F32) + col_send(own, H_SWAP).astype(F32)).astype(BF16)
    far = col_send(own, y_step(2))
    prv = col_send(own, y_step(1))
    nxt = col_send(own, y_step(-1))
    mine = y_joined(pos, (own, nxt, far, prv))
    return mine, col_send(mine, CORE_SWAP)


def activate(value):
    return jax.nn.gelu(value, approximate=True)


def activated(part, arrived):
    def kernel(part_ref, arrived_ref, active, slope):
        value, pull_back = jax.vjp(activate, part_ref[...] + arrived_ref[...].astype(F32))
        active[...] = value.astype(BF16)
        slope[...] = pull_back(jnp.ones_like(value))[0]

    return call(
        kernel, [VMEM] * 2, [VMEM] * 2,
        [jax.ShapeDtypeStruct(part.shape, BF16), jax.ShapeDtypeStruct(part.shape, F32)],
    )(part, arrived)


def body(inputs, up_weight, down_weight, up_mask, down_mask, cotangent):
    col = lax.axis_index("col")
    pos = jnp.stack([lax.axis_index("row") % 4, col // 2 % 4, col % 2]).astype(jnp.int32)
    far_a, far_b, masked_up = hidden_far(pos, up_mask, inputs, up_weight)
    hidden = z_reduce((far_a, far_b, *hidden_near(pos, inputs, masked_up)))
    active_own, slope = activated(hidden, x_swap(hidden))
    active = z_collect(active_own)
    grad = z_reduce(grad_part(pos, down_mask, cotangent, down_weight))
    hidden_grad = z_collect(((grad + x_swap(grad).astype(F32)) * slope).astype(BF16))
    output_halves = col_reduce(pos, *down_part(pos, down_mask, active, down_weight, False))
    input_halves = col_reduce(pos, *down_part(pos, up_mask, hidden_grad, up_weight, True))
    down_grad = down_gradient(pos, down_mask, active, cotangent)
    up_grad = up_gradient(pos, up_mask, inputs, hidden_grad)
    output, input_grad = all_rows(pos, *output_halves, *input_halves)
    return (output, input_grad, up_grad, down_grad)


def solution(mesh):
    in_specs = (
        P(None, "row"),
        P("row", "col"),
        P("col", "row"),
        P("row", "col"),
        P("col", "row"),
        P(None, "row"),
    )
    out_specs = (P(None, "row"), P(None, "row"), P("row", "col"), P("col", "row"))
    return jax.shard_map(body, mesh=mesh, in_specs=in_specs, out_specs=out_specs, check_vma=False)
```
